128 devices in a mesh: tile: 8 (over z, core), lvl: 16 (over x, y).
Axes of the slice: x: 4, y: 4, z: 4, core: 2. Of those that a mesh axis runs over, the one named last changes fastest.
Arguments:
- parents: int32 [3, 1024, 4], P(None, ('tile', 'lvl')), may hold values from -1 to 3071, as said below
- factors: bfloat16 [3, 1024, 4, 256, 256], P(None, ('tile', 'lvl')), may hold values from -0.125 to 0.125
- chol: bfloat16 [4, 1024, 256, 256], P(None, ('tile', 'lvl')), as said below
- noise: bfloat16 [4, 1024, 256, 256], P(None, ('tile', 'lvl')), may hold values from -6 to 6
Outputs:
- samples: bfloat16 [4, 1024, 256, 256], P(None, ('tile', 'lvl'))
The draws below stay inside these ranges and needn't reach their ends.
Inputs may be any that keep to these rules, and one draw needn't show every extreme that they name: `parents`: parents of a block of level s + 1 are blocks of levels 0 to s owned by a device of the same spatial tile or of the tile with index one less. Among the 32 entries of one device's blocks of one level, at most 2 name blocks owned by any one device of the same tile and at most 1 name blocks owned by any one device of the previous tile; in every draw, both bounds are reached by some device (devices of tile 0 have no previous tile, so their previous-tile entries are -1). `chol`: lower triangular with a positive diagonal.
All inputs are finite; a program needn't handle non-finite values.
Results may differ from the reference program's by a relative error of at most 0.0032.
Values may be sent and summed in bfloat16 or wider, within the bound.
A program may use at most 128 MiB of HBM per device.

```python
import jax
import jax.numpy as jnp
from jax import lax

BLOCK = 256
REAL = 256
NPAR = 4
LEVELS = 4
CAP = 2
CAPX = 1
KB = 8
PEERS = 16
NB = 1024


def draw_parents(key, part):
    device_count = NB // KB
    ref_count = KB * NPAR
    position_count = PEERS * (CAP + CAPX)

    def one_list(section, device):
        base = jax.random.fold_in(jax.random.fold_in(key, section + 11), device)
        keys = jax.random.split(base, 7)
        own_tile = device // PEERS
        shuffled = jax.random.permutation(keys[0], position_count)
        forced_same = jax.random.randint(keys[1], (), 0, PEERS)
        forced_prior = jax.random.randint(keys[2], (), 0, PEERS)
        positions = jnp.arange(position_count)
        forced = (positions // CAP == forced_same) & (positions < PEERS * CAP) | (positions == PEERS * CAP + forced_prior * CAPX)
        scores = jnp.where(forced, -1, shuffled)
        picked = jnp.argsort(scores, stable=True)[:ref_count]
        picked_forced = forced[picked]
        spread = jax.random.permutation(keys[3], ref_count)
        chosen = picked[spread]
        chosen_forced = picked_forced[spread]
        from_prior = chosen >= PEERS * CAP
        owner_lane = jnp.where(from_prior, (chosen - PEERS * CAP) // CAPX, chosen // CAP)
        owner_tile = own_tile - from_prior.astype(jnp.int32)
        parent_level = jax.random.randint(keys[4], (ref_count,), 0, section + 1)
        within = jax.random.randint(keys[5], (ref_count,), 0, KB)
        dropped = (jax.random.randint(keys[6], (ref_count,), 0, 4) == 0) & jnp.logical_not(chosen_forced)
        usable = (owner_tile >= 0) & jnp.logical_not(dropped)
        block_id = parent_level * NB + (owner_tile * PEERS + owner_lane) * KB + within
        return jnp.where(usable, block_id, -1).astype(jnp.int32).reshape(KB, NPAR)
    lists = jax.vmap(jax.vmap(one_list, (None, 0)), (0, None))(jnp.arange(LEVELS - 1), jnp.arange(device_count))
    return lists.reshape(LEVELS - 1, NB, NPAR)


def draw_chol(key, part):
    key_off, key_diag = jax.random.split(jax.random.fold_in(key, 5))
    off_scale = 0.6
    diag_part = jax.random.uniform(key_diag, (LEVELS, NB, BLOCK), jnp.float32, 0.5, 1.5)
    off_part = jax.random.normal(key_off, (LEVELS, NB, BLOCK, BLOCK), jnp.float32) * (off_scale / BLOCK ** 0.5)
    row_index = jnp.arange(BLOCK)[:, None]
    col_index = jnp.arange(BLOCK)[None, :]
    lower = jnp.where(row_index > col_index, off_part, 0.0)
    diagonal = jnp.where(row_index == col_index, diag_part[..., None], 0.0)
    return (lower + diagonal).astype(jnp.bfloat16)


def shard_levels(rng, shape, pieces, smallest, largest):
    loudness, own = 1.0, jax.random.fold_in(rng, 6)
    for axis_at, parts in pieces:
        steps = jnp.exp(jax.random.uniform(jax.random.fold_in(own, axis_at), (parts,), jnp.float32, smallest / len(pieces), largest / len(pieces)))
        loudness = loudness * jnp.repeat(steps, shape[axis_at] // parts).reshape([-1 if axis == axis_at else 1 for axis in range(len(shape))])
    return loudness


def centred(own_key, shape, width, most, pieces=(), held_as=jnp.bfloat16):
    values = jax.random.normal(own_key, shape, jnp.float32) * width
    if len(pieces) > 0:
        values = shard_levels(own_key, shape, pieces, -0.22, 0.18) * values
    return jnp.clip(values, min=-most, max=most).astype(held_as)


def setup_inputs(seed: int = 0) -> dict:
    key_list = jax.random.split(jax.random.key(seed), 5)
    return {
        "parents": draw_parents(jax.random.fold_in(key_list[4], 71), 0),
        "factors": centred(key_list[1], (LEVELS - 1, NB, NPAR, BLOCK, BLOCK), (8 * BLOCK) ** -0.5, 0.125, ((1, 128),)),
        "chol": draw_chol(jax.random.fold_in(key_list[4], 71), 0),
        "noise": centred(key_list[3], (LEVELS, NB, BLOCK, REAL), 1.0, 6.0, ((1, 128),)),
    }


def reference(parents, factors, chol, noise):
    total_blocks = chol.shape[1]

    def first_block(pair):
        return jnp.dot(pair[0], pair[1], preferred_element_type=jnp.float32).astype(jnp.bfloat16)

    level_zero = lax.map(first_block, (chol[0], noise[0]))
    samples = jnp.zeros((LEVELS, total_blocks, BLOCK, REAL), jnp.bfloat16)
    samples = samples.at[0].set(level_zero)
    for section in range(1, LEVELS):
        flat_samples = samples.reshape(LEVELS * total_blocks, BLOCK, REAL)

        def one_block(items):
            block_ids, amats, lower, draws = items
            total = jnp.dot(lower, draws, preferred_element_type=jnp.float32)
            for slot in range(NPAR):
                where_from = jnp.maximum(block_ids[slot], 0).astype(jnp.int32)
                parent_block = lax.dynamic_index_in_dim(flat_samples, where_from, 0, keepdims=False)
                term = jnp.dot(amats[slot], parent_block, preferred_element_type=jnp.float32)
                total = total + jnp.where(block_ids[slot] >= 0, term, jnp.zeros_like(term))
            return total.astype(jnp.bfloat16)

        level_out = lax.map(one_block, (parents[section - 1], factors[section - 1], chol[section], noise[section]))
        samples = samples.at[section].set(level_out)
    return samples
```

```python
import functools

import jax
import jax.numpy as jnp
from jax import lax
from jax.experimental import pallas as pl
from jax.experimental.pallas import tpu as pltpu
from jax.sharding import PartitionSpec as P

MESH = pl.DeviceIdType.MESH
NPAR = 4
CAP = 2
CAPX = 1
SLOTS = CAP + CAPX
SIDE = 4
FAR = (1, 3, 2)


def kernel(
    dims, req_ref, pos_ref, fac_ref, chol_ref, noise_ref, out_ref,
    held, got, cross, sent, passed, fac, low, draw, base, last,
    lists, table, g1s, g1r, g2s, g2r, hs, hr, xs, xr, fs, cs, cr,
    list_s, list_r, load_sem, out_sem, table_sem,
):
    depth, blocks, rows, half, tiles, span = dims
    tile = lax.axis_index("tile")
    lane = lax.axis_index("lvl")
    ix, iy = lane // SIDE, lane % SIDE

    def at(dx, dy):
        return ((ix + dx) % SIDE) * SIDE + (iy + dy) % SIDE

    def along(route, d):
        return {"lvl": at(d, 0) if route == 0 else at(0, d)}

    def across(route, d):
        return along(1 - route, d)

    def remote(src, dst, ssem, rsem, device):
        return pltpu.make_async_remote_copy(
            src_ref=src, dst_ref=dst, send_sem=ssem, recv_sem=rsem,
            device_id=device, device_id_type=MESH,
        )

    def arrived(ref, sem):
        remote(ref, ref, sem, sem, along(0, 1)).wait_recv()

    def gone(ref, sem):
        remote(ref, ref, sem, sem, along(0, 1)).wait_send()

    def load_level(level):
        p = level % 2
        return (
            pltpu.make_async_copy(chol_ref.at[level], low.at[p], load_sem.at[p]),
            pltpu.make_async_copy(noise_ref.at[level], draw.at[p], load_sem.at[2 + p]),
        )

    def load_factors(section):
        return pltpu.make_async_copy(fac_ref.at[section - 1], fac, load_sem.at[4])

    for level in (0, 1):
        for copy in load_level(level):
            copy.start()
    load_factors(1).start()

    barrier = pltpu.get_barrier_semaphore()
    for route in range(2):
        for d in FAR:
            pl.semaphore_signal(barrier, inc=1, device_id=across(route, d), device_id_type=MESH)

    @pl.when(tile > 0)
    def _():
        pl.semaphore_signal(barrier, inc=1, device_id={"tile": tile - 1}, device_id_type=MESH)

    @pl.when(tile < tiles - 1)
    def _():
        pl.semaphore_signal(barrier, inc=1, device_id={"tile": tile + 1}, device_id_type=MESH)

    ends = (tile > 0).astype(jnp.int32) + (tile < tiles - 1).astype(jnp.int32)
    pl.semaphore_wait(barrier, 6 + ends)

    @pl.when(tile > 0)
    def _():
        remote(
            req_ref, lists.at[1], list_s.at[0], list_r.at[0], {"tile": tile - 1}
        ).start()

    def peer(route, d):
        return 1 + 3 * route + FAR.index(d)

    def send_list(src, which):
        for route in range(2):
            for d in FAR:
                mine, theirs = peer(route, d), peer(route, SIDE - d)
                remote(
                    src, lists.at[2 * theirs + which], list_s.at[2 * mine + which],
                    list_r.at[2 * theirs + which], across(route, d),
                ).start()

    send_list(req_ref, 0)

    def spread(level, k):
        p = level % 2
        for route in range(2):
            for way, (d, o) in enumerate(((1, 1), (3, 3))):
                remote(
                    held[level][route][0].at[k], held[level][route][o].at[k],
                    g1s.at[p, route, way, k], g1r.at[p, route, way, k], along(route, d),
                ).start()

    def keep(level, k, total):
        value = total.astype(jnp.bfloat16)
        if level < depth - 1:
            held[level][0][0][k] = value[:, :half]
            held[level][1][0][k] = value[:, half:]

            @pl.when(k > 0)
            def _():
                spread(level, k - 1)
        else:
            last[k] = value

    def product(level, k):
        p = level % 2
        return jnp.dot(low[p, k], draw[p, k], preferred_element_type=jnp.float32)

    for copy in load_level(0):
        copy.wait()

    def first(k, carry):
        keep(0, k, product(0, k))
        return carry

    lax.fori_loop(0, blocks, first, 0)
    for copy in load_level(2):
        copy.start()
    spread(0, blocks - 1)

    lists[0] = req_ref[...]

    @pl.when(tile < tiles - 1)
    def _():
        arrived(lists.at[1], list_r.at[0])

    @pl.when(tile == tiles - 1)
    def _():
        lists[1] = req_ref[...]

    send_list(lists.at[1], 1)
    for route in range(2):
        for d in FAR:
            for which in range(2):
                n = 2 * peer(route, d) + which
                arrived(lists.at[n], list_r.at[n])
    copy = pltpu.make_async_copy(lists, table, table_sem)
    copy.start()
    copy.wait()

    def owner(route, o):
        column = at(-o, 0) if route == 0 else at(0, -o)
        return column * SLOTS

    def pick(section, route, o, wanted):
        within = wanted % blocks
        value = held[0][route][o][within]
        for level in range(1, section):
            value = jnp.where(
                wanted >= level * blocks, held[level][route][o][within], value
            )
        return value

    def wanted_at(section, n, route, o, slot):
        which = 0 if slot < CAP else 1
        return table[2 * n + which, section - 1, owner(route, o) + slot]

    def to_next(section, route, so, o, start):
        p = section % 2
        place = (so * SIDE + o) * SLOTS + CAP
        copy = remote(
            got[p][route].at[pl.ds(place, CAPX)],
            cross[section - 1][route].at[pl.ds(so * SIDE + o, CAPX)],
            cs.at[route, so, o], cr.at[section - 1, route, so, o], {"tile": tile + 1},
        )

        @pl.when(tile < tiles - 1)
        def _():
            if start:
                copy.start()
            else:
                copy.wait_send()

    PARTS = ((CAP, CAPX), (0, CAP))

    def hand(section, route, o, finish=False):
        p = section % 2
        for part, (begin, count) in enumerate(PARTS):
            for i, d in ((2, 2), (0, 1), (1, 3)):
                src = sent[route].at[pl.ds((i * SIDE + o) * SLOTS + begin, count)]
                if d == 2:
                    towards = 1 if o < 2 else 3
                    dst = passed[p][route].at[pl.ds(o * SLOTS + begin, count)]
                    rsem = xr.at[p, route, o, part]
                else:
                    towards = d
                    dst = got[p][route].at[pl.ds((d * SIDE + o) * SLOTS + begin, count)]
                    rsem = hr.at[p, route, d, o, part]
                copy = remote(src, dst, hs.at[route, i, o, part], rsem, across(route, towards))
                if finish:
                    copy.wait_send()
                else:
                    copy.start()

    def build(section, route, o):
        p = section % 2

        def one(i, carry):
            for slot in range(SLOTS):
                sent[route][(i * SIDE + o) * SLOTS + slot] = pick(
                    section, route, o, wanted_at(section, 1 + 3 * route + i, route, o, slot)
                )
            return carry

        lax.fori_loop(0, 3, one, 0)
        for slot in range(SLOTS):
            got[p][route][o * SLOTS + slot] = pick(
                section, route, o, wanted_at(section, 0, route, o, slot)
            )

    def relay(section, route, o, finish=False):
        p = section % 2
        towards = 1 if o < 2 else 3
        for part, (begin, count) in enumerate(PARTS):
            src = passed[p][route].at[pl.ds(o * SLOTS + begin, count)]
            copy = remote(
                src, got[p][route].at[pl.ds((2 * SIDE + o) * SLOTS + begin, count)],
                xs.at[route, o, part], hr.at[p, route, 2, o, part], across(route, towards),
            )
            if finish:
                copy.wait_send()
            else:
                arrived(src, xr.at[p, route, o, part])
                copy.start()

    def onward(section, route, so, o):
        p = section % 2
        place = (so * SIDE + o) * SLOTS + CAP
        arrived(got[p][route].at[pl.ds(place, CAPX)], hr.at[p, route, so, o, 0])
        to_next(section, route, so, o, True)

    def forward(level, k, start):
        p = level % 2
        for route in range(2):
            for way, (d, o) in enumerate(((1, 1), (3, 3))):
                block = 2 * k + way
                src = held[level][route][o].at[block]
                if start:
                    arrived(src, g1r.at[p, route, way, block])
                copy = remote(
                    src, held[level][route][2].at[block], g2s.at[p, route, way, k],
                    g2r.at[p, route, way, k], along(route, d),
                )
                if start:
                    copy.start()
                else:
                    copy.wait_send()

    def drain(section):
        for route in range(2):
            for o in range(SIDE):
                hand(section, route, o, finish=True)
                relay(section, route, o, finish=True)
                for so in range(SIDE):
                    to_next(section, route, so, o, False)

    def output(level):
        return [
            pltpu.make_async_copy(
                held[level][route][0],
                out_ref.at[level, :, :, pl.ds(route * half, half)],
                out_sem.at[2 * level + route],
            )
            for route in range(2)
        ]

    for section in range(1, depth):
        level = section - 1
        p = level % 2
        q = section % 2
        if section > 1:
            drain(section - 1)
        for route in range(2):
            build(section, route, 0)
            if route == 1:
                hand(section, 0, 0)
        hand(section, 1, 0)
        for route in range(2):
            to_next(section, route, 0, 0, True)

        for copy in load_level(section):
            copy.wait()

        def own(k, carry):
            base[k] = product(section, k)
            return carry

        lax.fori_loop(0, blocks, own, 0)
        if section + 2 < depth and section > 0:
            for copy in load_level(section + 2):
                copy.start()

        def pass_on(k, carry):
            forward(level, k, True)
            return carry

        lax.fori_loop(0, blocks // 2, pass_on, 0)

        def rest(k, carry):
            for route in range(2):
                arrived(held[level][route][1].at[2 * k + 1], g1r.at[p, route, 0, 2 * k + 1])
                arrived(held[level][route][3].at[2 * k], g1r.at[p, route, 1, 2 * k])
            return carry

        lax.fori_loop(0, blocks // 2, rest, 0)
        for o in (1, 3):
            for route in range(2):
                build(section, route, o)
            for route in range(2):
                hand(section, route, o)
                to_next(section, route, 0, o, True)
        for route in range(2):
            relay(section, route, 0)
        for route in range(2):
            for so in (1, 3):
                onward(section, route, so, 0)

        def second(k, carry):
            for route in range(2):
                for way in range(2):
                    arrived(
                        held[level][route][2].at[2 * k + way], g2r.at[p, route, way, k]
                    )
            return carry

        lax.fori_loop(0, blocks // 2, second, 0)
        for route in range(2):
            build(section, route, 2)
        for route in range(2):
            hand(section, route, 2)
            to_next(section, route, 0, 2, True)
        for o in (1, 3, 2):
            for route in range(2):
                relay(section, route, o)
        for copy in output(level):
            copy.start()
        for route in range(2):
            onward(section, route, 2, 0)
        for o in (1, 3, 2):
            for so in (1, 3, 2):
                for route in range(2):
                    onward(section, route, so, o)

        def sent_all(k, carry):
            for route in range(2):
                for way in range(2):
                    gone(held[level][route][0].at[k], g1s.at[p, route, way, k])
            return carry

        lax.fori_loop(0, blocks, sent_all, 0)

        def forwarded(k, carry):
            forward(level, k, False)
            return carry

        lax.fori_loop(0, blocks // 2, forwarded, 0)
        for route in range(2):
            for o in range(SIDE):
                for so in range(1, SIDE):
                    place = (so * SIDE + o) * SLOTS
                    arrived(got[q][route].at[pl.ds(place, CAP)], hr.at[q, route, so, o, 1])

        @pl.when(tile > 0)
        def _():
            for route in range(2):
                for o in range(SIDE):
                    for so in range(SIDE):
                        place = so * SIDE + o
                        arrived(
                            cross[section - 1][route].at[pl.ds(place, CAPX)],
                            cr.at[section - 1, route, so, o],
                        )

        load_factors(section).wait()

        def mix(k, carry):
            total = base[k]
            for slot in range(NPAR):
                code = pos_ref[section - 1, k * NPAR + slot]
                kind = code // 65536
                halves = []
                for route in range(2):
                    place = code % 256 if route == 0 else (code // 256) % 256
                    same = got[q][route][place % (SIDE * SIDE * SLOTS)]
                    prior = cross[section - 1][route][(place // SLOTS) % (SIDE * SIDE)]
                    value = jnp.where(kind == 2, prior, same)
                    halves.append(jnp.where(kind == 0, jnp.zeros_like(value), value))
                parent = jnp.concatenate(halves, axis=1)
                total = total + jnp.dot(
                    fac[k, slot], parent, preferred_element_type=jnp.float32
                )
            keep(section, k, total)
            if section == depth - 1:

                @pl.when(k > 0)
                def _():
                    write_last(k - 1).start()

            return carry

        def write_last(k):
            return pltpu.make_async_copy(
                last.at[k], out_ref.at[depth - 1, k], out_sem.at[2 * depth - 2 + k]
            )

        lax.fori_loop(0, blocks, mix, 0)
        if section < depth - 1:
            load_factors(section + 1).start()
            spread(section, blocks - 1)
        else:
            write_last(blocks - 1).start()

    drain(depth - 1)

    @pl.when(tile > 0)
    def _():
        gone(req_ref, list_s.at[0])

    for route in range(2):
        for d in FAR:
            for which in range(2):
                gone(req_ref, list_s.at[2 * peer(route, d) + which])
    for level in range(depth - 1):
        for copy in output(level):
            copy.wait()
    for k in range(blocks):
        pltpu.make_async_copy(
            last.at[k], out_ref.at[depth - 1, k], out_sem.at[2 * depth - 2 + k]
        ).wait()


def tables(parents, own_tile, lane, peers, blocks, total):
    sections = parents.shape[0]
    ids = parents.reshape(sections, -1)
    count = ids.shape[1]
    valid = ids >= 0
    ids = jnp.maximum(ids, 0)
    level, block = ids // total, ids % total
    device = block // blocks
    owner = device % peers
    prior = valid & (device // peers != own_tile)
    local = level * blocks + block % blocks
    group = jnp.where(valid, owner + peers * prior.astype(jnp.int32), -1)
    earlier = jnp.arange(count)[:, None] > jnp.arange(count)[None, :]
    rank = jnp.sum((group[:, :, None] == group[:, None, :]) & earlier, axis=2, dtype=jnp.int32)
    slot = jnp.where(prior, CAP, jnp.minimum(rank, CAP - 1))
    column = jnp.where(valid, owner * SLOTS + slot, -1)
    hits = column[:, None, :] == jnp.arange(128)[None, :, None]
    asked = jnp.sum(jnp.where(hits, local[:, None, :], 0), axis=2, dtype=jnp.int32)
    asked = jnp.concatenate([asked, jnp.zeros((8 - sections, 128), jnp.int32)])
    dx = (lane // SIDE - owner // SIDE) % SIDE
    dy = (lane % SIDE - owner % SIDE) % SIDE
    first = (dy * SIDE + dx) * SLOTS + slot
    second = (dx * SIDE + dy) * SLOTS + slot
    kind = jnp.where(valid, 1 + prior.astype(jnp.int32), 0)
    return asked, first + 256 * second + 65536 * kind


def shards(parents, factors, chol, noise):
    peers = lax.axis_size("lvl")
    tiles = lax.axis_size("tile")
    depth, blocks, rows, _ = chol.shape
    real = noise.shape[3]
    half = real // 2
    span = SIDE * SIDE
    asked, places = tables(
        parents, lax.axis_index("tile"), lax.axis_index("lvl"), peers, blocks,
        blocks * peers * tiles,
    )

    def vmem(*shape, dtype=jnp.bfloat16):
        return pltpu.VMEM(shape, dtype)

    dma = pltpu.SemaphoreType.DMA
    scratch = [
        [[[vmem(blocks, rows, half) for _ in range(SIDE)] for _ in range(2)] for _ in range(depth - 1)],
        [[vmem(span * SLOTS, rows, half) for _ in range(2)] for _ in range(2)],
        [[vmem(span, rows, half) for _ in range(2)] for _ in range(depth - 1)],
        [vmem(3 * SIDE * SLOTS, rows, half) for _ in range(2)],
        [[vmem(SIDE * SLOTS, rows, half) for _ in range(2)] for _ in range(2)],
        vmem(blocks, NPAR, rows, rows),
        vmem(2, blocks, rows, rows),
        vmem(2, blocks, rows, real),
        vmem(blocks, rows, real, dtype=jnp.float32),
        vmem(blocks, rows, real),
        vmem(14, 8, 128, dtype=jnp.int32),
        pltpu.SMEM((14, 8, 128), jnp.int32),
        dma((2, 2, 2, blocks)), dma((2, 2, 2, blocks)),
        dma((2, 2, 2, blocks // 2)), dma((2, 2, 2, blocks // 2)),
        dma((2, 3, SIDE, 2)), dma((2, 2, SIDE, SIDE, 2)),
        dma((2, SIDE, 2)), dma((2, 2, SIDE, 2)),
        dma((1,)),
        dma((2, SIDE, SIDE)), dma((depth - 1, 2, SIDE, SIDE)),
        dma((14,)), dma((14,)),
        dma((5,)), dma((2 * depth - 2 + blocks,)), dma,
    ]
    flat, tree = jax.tree.flatten(scratch)

    def body(*refs):
        operands, rest = refs[:6], refs[6:]
        kernel(
            (depth, blocks, rows, half, tiles, span), *operands,
            *jax.tree.unflatten(tree, rest),
        )

    anywhere = pl.BlockSpec(memory_space=pl.ANY)
    return pl.pallas_call(
        body,
        out_shape=jax.ShapeDtypeStruct((depth, blocks, rows, real), jnp.bfloat16),
        in_specs=[
            pl.BlockSpec(memory_space=pltpu.VMEM),
            pl.BlockSpec(memory_space=pltpu.SMEM),
            anywhere, anywhere, anywhere,
        ],
        out_specs=anywhere,
        scratch_shapes=flat,
        compiler_params=pltpu.CompilerParams(
            collective_id=0, has_side_effects=True, vmem_limit_bytes=67043328
        ),
        name="field",
    )(asked, places, factors, chol, noise)


def solution(mesh):
    placed = (
        P(None, ("tile", "lvl"), None),
        P(None, ("tile", "lvl"), None, None, None),
        P(None, ("tile", "lvl"), None, None),
        P(None, ("tile", "lvl"), None, None),
    )
    return jax.shard_map(
        shards,
        mesh=mesh,
        in_specs=placed,
        out_specs=P(None, ("tile", "lvl"), None, None),
        check_vma=False,
    )
```

```python
import jax
import jax.numpy as jnp
from jax import lax
from jax.experimental import pallas as pl
from jax.experimental.pallas import tpu as pltpu
from jax.sharding import PartitionSpec as P

MESH = pl.DeviceIdType.MESH
NPAR = 4
CAP = 2
SIDE = 4
FAR = (2, 1, 3)
PIECES = 2


def kernel(
    dims, parents, fac_ref, chol_ref, noise_ref, out_ref,
    held, got, cross, sent_same, sent_next, fac, low, draw, base, last,
    asked, lists, table, codes, g1s, g1r, g2s, g2r, hs, hr, cs, cr,
    list_s, list_r, load_sem, out_sem, table_sem,
):
    depth, blocks, rows, real, tiles = dims
    tall, wide = rows // 2, real // 2
    piece = blocks // PIECES
    peers = SIDE * SIDE
    total_blocks = blocks * peers * tiles
    tile = lax.axis_index("tile")
    lane = lax.axis_index("lvl")
    ix, iy = lane // SIDE, lane % SIDE
    has_prior = tile > 0
    has_next = tile < tiles - 1

    def at(dx, dy):
        return ((ix + dx) % SIDE) * SIDE + (iy + dy) % SIDE

    def along(route, d):
        return at(d, 0) if route == 0 else at(0, d)

    def across(route, d):
        return along(1 - route, d)

    def remote(src, dst, ssem, rsem, device):
        return pltpu.make_async_remote_copy(
            src_ref=src, dst_ref=dst, send_sem=ssem, recv_sem=rsem,
            device_id=device, device_id_type=MESH,
        )

    def arrived(ref, sem):
        remote(ref, ref, sem, sem, {"lvl": at(1, 0)}).wait_recv()

    def load_level(level):
        p = level % 2
        return (
            pltpu.make_async_copy(chol_ref.at[level], low.at[p], load_sem.at[p]),
            pltpu.make_async_copy(noise_ref.at[level], draw.at[p], load_sem.at[2 + p]),
        )

    def load_factors(section):
        return pltpu.make_async_copy(fac_ref.at[section - 1], fac, load_sem.at[4])

    for level in (0, 1):
        for copy in load_level(level):
            copy.start()
    load_factors(1).start()

    barrier = pltpu.get_barrier_semaphore()

    def greet(device):
        pl.semaphore_signal(barrier, inc=1, device_id=device, device_id_type=MESH)

    for route in range(2):
        for d in FAR:
            greet({"lvl": across(route, d)})

    @pl.when(has_prior)
    def _():
        greet({"tile": tile - 1})
        for route in range(2):
            for d in FAR:
                greet({"tile": tile - 1, "lvl": across(route, d)})

    @pl.when(has_next)
    def _():
        greet({"tile": tile + 1})
        for route in range(2):
            for d in FAR:
                greet({"tile": tile + 1, "lvl": across(route, d)})

    def entry(section, n):
        number = parents[section - 1, n // NPAR, n % NPAR]
        clipped = jnp.maximum(number, 0)
        block = lax.rem(clipped, total_blocks)
        device = lax.div(block, blocks)
        local = lax.div(clipped, total_blocks) * blocks + lax.rem(block, blocks)
        return number >= 0, lax.div(device, peers) != tile, lax.rem(device, peers), local

    row = lax.broadcasted_iota(jnp.int32, (8, 128), 0)
    column = lax.broadcasted_iota(jnp.int32, (8, 128), 1)

    def ask(section):
        def one(n, carry):
            one_slot, two_slot, prior_slot = carry
            valid, prior, owner, local = entry(section, n)
            place = jnp.where(valid, jnp.where(prior, peers, 0) + owner, -1)
            here = (row == section - 1) & (column == place)
            there = (row == section - 1) & (column + peers == place) & (column < peers)
            here = here & (column < peers)
            two_slot = jnp.where(here & (one_slot >= 0), local, two_slot)
            one_slot = jnp.where(here & (one_slot < 0), local, one_slot)
            return one_slot, two_slot, jnp.where(there, local, prior_slot)

        return one

    state = (jnp.full((8, 128), -1, jnp.int32),) * 3
    for section in range(1, depth):
        state = lax.fori_loop(0, blocks * NPAR, ask(section), state)
    for slot in range(3):
        asked[slot] = jnp.maximum(state[slot], 0)

    ends = has_prior.astype(jnp.int32) + has_next.astype(jnp.int32)
    pl.semaphore_wait(barrier, 6 + 7 * ends)

    def peer(route, d):
        return 1 + 3 * route + FAR.index(d)

    def list_copies(which):
        moves = []
        if which == 1:
            moves.append((0, 0, {"tile": tile - 1}))
        for route in range(2):
            for d in FAR:
                device = {"lvl": across(route, d)}
                if which == 1:
                    device["tile"] = tile - 1
                moves.append((peer(route, d), peer(route, SIDE - d), device))
        return [
            remote(
                asked, lists.at[7 * which + theirs], list_s.at[7 * which + mine],
                list_r.at[7 * which + theirs], device,
            )
            for mine, theirs, device in moves
        ]

    for copy in list_copies(0):
        copy.start()

    @pl.when(has_prior)
    def _():
        for copy in list_copies(1):
            copy.start()

    WAYS = ((1, 1), (3, 3))

    def part(k):
        return pl.ds(k * piece, piece)

    def spread(level, chain, k):
        p = level % 2
        for route in range(2):
            own = held[level][chain][route]
            for way, (d, o) in enumerate(WAYS):
                remote(
                    own[0].at[part(k)], own[o].at[part(k)],
                    g1s.at[p, chain, route, way, k], g1r.at[p, chain, route, way, k],
                    {"lvl": along(route, d)},
                ).start()

    def forward(level, chain, start):
        p = level % 2
        for way, (d, o) in enumerate(WAYS):
            for route in range(2):
                own = held[level][chain][route]
                src = own[o].at[part(way)]
                if start:
                    arrived(src, g1r.at[p, chain, route, way, way])
                copy = remote(
                    src, own[2].at[part(way)], g2s.at[p, chain, route, way],
                    g2r.at[p, chain, route, way], {"lvl": along(route, d)},
                )
                if start:
                    copy.start()
                else:
                    copy.wait_send()

    def gathered(level, chain):
        p = level % 2
        for route in range(2):
            own = held[level][chain][route]
            for way, (d, o) in enumerate(WAYS):
                arrived(own[o].at[part(1 - way)], g1r.at[p, chain, route, way, 1 - way])
                arrived(own[2].at[part(way)], g2r.at[p, chain, route, way])

    def sent_on(level, chain):
        p = level % 2
        for route in range(2):
            own = held[level][chain][route]
            for way, (d, o) in enumerate(WAYS):
                for k in range(PIECES):
                    remote(
                        own[0].at[part(k)], own[0].at[part(k)],
                        g1s.at[p, chain, route, way, k], g1s.at[p, chain, route, way, k],
                        {"lvl": along(route, d)},
                    ).wait_send()
        forward(level, chain, False)

    def keep(level, chain, k, value):
        held[level][chain][0][0][k] = value[:tall]
        held[level][chain][1][0][k] = value[tall:]

    def product(level, k):
        p = level % 2
        return jnp.dot(low[p, k], draw[p, k], preferred_element_type=jnp.float32)

    for copy in load_level(0):
        copy.wait()

    def first(k, carry):
        value = product(0, k).astype(jnp.bfloat16)
        for chain in range(2):
            keep(0, chain, k, value[:, chain * wide : (chain + 1) * wide])
        return carry

    lax.fori_loop(0, piece, first, 0)
    spread(0, 0, 0)
    lax.fori_loop(piece, blocks, first, 0)
    for copy in load_level(2):
        copy.start()
    spread(0, 0, 1)
    for k in range(PIECES):
        spread(0, 1, k)

    def owner_lane(route, o):
        return at(-o, 0) if route == 0 else at(0, -o)

    def pick(section, chain, route, o, wanted):
        within = lax.rem(wanted, blocks)
        value = held[0][chain][route][o][within]
        for level in range(1, section):
            value = jnp.where(
                wanted >= level * blocks, held[level][chain][route][o][within], value
            )
        return value

    def build(section, chain, route):
        p = section % 2

        def one(i, carry):
            n = jnp.where(i == 3, 0, 1 + 3 * route + i)
            for o in range(SIDE):
                source = owner_lane(route, o)
                sent_next[chain][route][i * SIDE + o] = pick(
                    section, chain, route, o, table[7 + n, 2, section - 1, source]
                )
                for slot in range(CAP):
                    sent_same[chain][route][(i * SIDE + o) * CAP + slot] = pick(
                        section, chain, route, o, table[n, slot, section - 1, source]
                    )
            return carry

        lax.fori_loop(0, 3, one, 0)
        for o in range(SIDE):
            source = owner_lane(route, o)
            sent_next[chain][route][3 * SIDE + o] = pick(
                section, chain, route, o, table[7, 2, section - 1, source]
            )
            for slot in range(CAP):
                got[p][chain][route][o * CAP + slot] = pick(
                    section, chain, route, o, table[0, slot, section - 1, source]
                )

    def hand_next(section, chain, route, start):
        @pl.when(has_next)
        def _():
            for i, d in enumerate(FAR + (0,)):
                device = {"tile": tile + 1}
                if d:
                    device["lvl"] = across(route, d)
                copy = remote(
                    sent_next[chain][route].at[pl.ds(i * SIDE, SIDE)],
                    cross[section - 1][chain][route].at[pl.ds(d * SIDE, SIDE)],
                    cs.at[chain, route, d], cr.at[section - 1, chain, route, d], device,
                )
                if start:
                    copy.start()
                else:
                    copy.wait_send()

    def hand_same(section, chain, route, start):
        p = section % 2
        size = SIDE * CAP
        for i, d in enumerate(FAR):
            copy = remote(
                sent_same[chain][route].at[pl.ds(i * size, size)],
                got[p][chain][route].at[pl.ds(d * size, size)],
                hs.at[chain, route, d], hr.at[p, chain, route, d],
                {"lvl": across(route, d)},
            )
            if start:
                copy.start()
            else:
                copy.wait_send()

    def received(section, chain):
        p = section % 2
        size = SIDE * CAP
        for route in range(2):
            for d in FAR:
                arrived(
                    got[p][chain][route].at[pl.ds(d * size, size)], hr.at[p, chain, route, d]
                )

        @pl.when(has_prior)
        def _():
            for route in range(2):
                for d in range(SIDE):
                    arrived(
                        cross[section - 1][chain][route].at[pl.ds(d * SIDE, SIDE)],
                        cr.at[section - 1, chain, route, d],
                    )

    def output(level):
        return [
            pltpu.make_async_copy(
                held[level][chain][route][0],
                out_ref.at[level, :, pl.ds(route * tall, tall), pl.ds(chain * wide, wide)],
                out_sem.at[level, chain, route],
            )
            for chain in range(2)
            for route in range(2)
        ]

    def write_last(chain, k):
        columns = pl.ds(chain * wide, wide)
        return pltpu.make_async_copy(
            last.at[part(k), :, columns], out_ref.at[depth - 1, part(k), :, columns],
            out_sem.at[depth - 1, chain, k],
        )

    def mix(section, chain):
        p = section % 2

        def one(k, carry):
            total = base[k, :, chain * wide : (chain + 1) * wide]
            for slot in range(NPAR):
                code = codes[section - 1, k * NPAR + slot]
                kind = lax.div(code, 65536)
                halves = []
                for route in range(2):
                    place = lax.rem(code if route == 0 else lax.div(code, 256), 256)
                    same = got[p][chain][route][lax.rem(place, CAP * peers)]
                    prior = cross[section - 1][chain][route][lax.rem(lax.div(place, CAP), peers)]
                    value = jnp.where(kind == 2, prior, same)
                    halves.append(jnp.where(kind == 0, jnp.zeros_like(value), value))
                parent = jnp.concatenate(halves, axis=0)
                total = total + jnp.dot(
                    fac[k, slot], parent, preferred_element_type=jnp.float32
                )
            value = total.astype(jnp.bfloat16)
            if section < depth - 1:
                keep(section, chain, k, value)
            else:
                last[k, :, chain * wide : (chain + 1) * wide] = value
            return carry

        return one

    for section in range(1, depth):
        level = section - 1
        for chain in range(2):
            forward(level, chain, True)
        if section == 1:
            lists[0] = asked[...]
            for route in range(2):
                for d in FAR:
                    arrived(asked, list_r.at[peer(route, d)])

            @pl.when(has_next)
            def _():
                for n in range(7):
                    arrived(asked, list_r.at[7 + n])

            @pl.when(jnp.logical_not(has_next))
            def _():
                for n in range(7):
                    lists[7 + n] = asked[...]

            copy = pltpu.make_async_copy(lists, table, table_sem)
            copy.start()
            copy.wait()
        for chain in range(2):
            if section > 1:
                for route in range(2):
                    hand_next(section - 1, chain, route, False)
                    hand_same(section - 1, chain, route, False)
            gathered(level, chain)
            for route in range(2):
                build(section, chain, route)
                if route == 1:
                    for r in range(2):
                        hand_next(section, chain, r, True)
                    for r in range(2):
                        hand_same(section, chain, r, True)

        if section == 1:

            def encode(n, carry):
                for s in range(1, depth):
                    valid, prior, owner, local = entry(s, n)
                    dx = lax.rem(ix - lax.div(owner, SIDE) + SIDE, SIDE)
                    dy = lax.rem(iy - lax.rem(owner, SIDE) + SIDE, SIDE)
                    slot = jnp.where(table[0, 0, s - 1, owner] == local, 0, 1)
                    near = (dy * SIDE + dx) * CAP + slot
                    turned = (dx * SIDE + dy) * CAP + slot
                    kind = jnp.where(valid, jnp.where(prior, 2, 1), 0)
                    codes[s - 1, n] = near + 256 * turned + 65536 * kind
                return carry

            lax.fori_loop(0, blocks * NPAR, encode, 0)

        for copy in load_level(section):
            copy.wait()

        def own(k, carry):
            base[k] = product(section, k)
            return carry

        lax.fori_loop(0, blocks, own, 0)
        if section + 2 < depth:
            for copy in load_level(section + 2):
                copy.start()
        for copy in output(level):
            copy.start()
        for chain in range(2):
            sent_on(level, chain)
        load_factors(section).wait()
        for chain in range(2):
            received(section, chain)
            for k in range(PIECES):
                lax.fori_loop(k * piece, (k + 1) * piece, mix(section, chain), 0)
                if section < depth - 1:
                    spread(section, chain, k)
                else:
                    write_last(chain, k).start()
        if section < depth - 1:
            load_factors(section + 1).start()

    for chain in range(2):
        for route in range(2):
            hand_next(depth - 1, chain, route, False)
            hand_same(depth - 1, chain, route, False)
    for copy in list_copies(0):
        copy.wait_send()

    @pl.when(has_prior)
    def _():
        for copy in list_copies(1):
            copy.wait_send()

    for level in range(depth - 1):
        for copy in output(level):
            copy.wait()
    for chain in range(2):
        for k in range(PIECES):
            write_last(chain, k).wait()


def shards(parents, factors, chol, noise):
    tiles = lax.axis_size("tile")
    depth, blocks, rows, _ = chol.shape
    real = noise.shape[3]
    peers = SIDE * SIDE

    def vmem(*shape, dtype=jnp.bfloat16):
        return pltpu.VMEM(shape, dtype)

    def half(count):
        return vmem(count, rows // 2, real // 2)

    def pairs(make):
        return [[make() for _ in range(2)] for _ in range(2)]

    dma = pltpu.SemaphoreType.DMA
    scratch = [
        [pairs(lambda: [half(blocks) for _ in range(SIDE)]) for _ in range(depth - 1)],
        [pairs(lambda: half(peers * CAP)) for _ in range(2)],
        [pairs(lambda: half(peers)) for _ in range(depth - 1)],
        pairs(lambda: half(3 * SIDE * CAP)),
        pairs(lambda: half(4 * SIDE)),
        vmem(blocks, NPAR, rows, rows),
        vmem(2, blocks, rows, rows),
        vmem(2, blocks, rows, real),
        vmem(blocks, rows, real, dtype=jnp.float32),
        vmem(blocks, rows, real),
        vmem(3, 8, 128, dtype=jnp.int32),
        vmem(14, 3, 8, 128, dtype=jnp.int32),
        pltpu.SMEM((14, 3, 8, 128), jnp.int32),
        pltpu.SMEM((depth - 1, blocks * NPAR), jnp.int32),
        dma((2, 2, 2, 2, PIECES)), dma((2, 2, 2, 2, PIECES)),
        dma((2, 2, 2, 2)), dma((2, 2, 2, 2)),
        dma((2, 2, SIDE)), dma((2, 2, 2, SIDE)),
        dma((2, 2, SIDE)), dma((depth - 1, 2, 2, SIDE)),
        dma((14,)), dma((14,)),
        dma((5,)), dma((depth, 2, 2)), dma,
    ]
    flat, tree = jax.tree.flatten(scratch)

    def body(*refs):
        operands, rest = refs[:5], refs[5:]
        kernel(
            (depth, blocks, rows, real, tiles), *operands, *jax.tree.unflatten(tree, rest)
        )

    anywhere = pl.BlockSpec(memory_space=pl.ANY)
    return pl.pallas_call(
        body,
        out_shape=jax.ShapeDtypeStruct((depth, blocks, rows, real), jnp.bfloat16),
        in_specs=[pl.BlockSpec(memory_space=pltpu.SMEM), anywhere, anywhere, anywhere],
        out_specs=anywhere,
        scratch_shapes=flat,
        compiler_params=pltpu.CompilerParams(
            collective_id=0, has_side_effects=True, vmem_limit_bytes=67043328
        ),
        name="field",
    )(parents, factors, chol, noise)


def solution(mesh):
    placed = (
        P(None, ("tile", "lvl"), None),
        P(None, ("tile", "lvl"), None, None, None),
        P(None, ("tile", "lvl"), None, None),
        P(None, ("tile", "lvl"), None, None),
    )
    return jax.shard_map(
        shards,
        mesh=mesh,
        in_specs=placed,
        out_specs=P(None, ("tile", "lvl"), None, None),
        check_vma=False,
    )
```

```python
import jax
import jax.numpy as jnp
from jax import lax
from jax.experimental import pallas as pl
from jax.experimental.pallas import tpu as pltpu
from jax.sharding import PartitionSpec as P

MESH = pl.DeviceIdType.MESH
NPAR = 4
CAP = 2
SIDE = 4
FAR = (2, 1, 3)
PIECES = 2


def kernel(
    dims, parents, fac_ref, chol_ref, noise_ref, out_ref,
    held, got, cross, passed, sent_same, sent_next, fac, low, draw, base, last,
    asked, lists, table, codes, g1s, g1r, g2s, g2r, hs, hr, cs, cr, ps, pr, qs, qr,
    list_s, list_r, load_sem, out_sem, table_sem,
):
    depth, blocks, rows, real, tiles = dims
    tall, wide = rows // 2, real // 2
    piece = blocks // PIECES
    peers = SIDE * SIDE
    planes = tiles // 2
    total_blocks = blocks * peers * tiles
    tile = lax.axis_index("tile")
    lane = lax.axis_index("lvl")
    ix, iy = lane // SIDE, lane % SIDE
    has_prior = tile > 0
    has_next = tile < tiles - 1

    def at(dx, dy):
        return ((ix + dx) % SIDE) * SIDE + (iy + dy) % SIDE

    def along(route, d):
        return at(d, 0) if route == 0 else at(0, d)

    def across(route, d):
        return along(1 - route, d)

    def remote(src, dst, ssem, rsem, device):
        return pltpu.make_async_remote_copy(
            src_ref=src, dst_ref=dst, send_sem=ssem, recv_sem=rsem,
            device_id=device, device_id_type=MESH,
        )

    def arrived(ref, sem):
        remote(ref, ref, sem, sem, {"lvl": at(1, 0)}).wait_recv()

    def load_level(level):
        p = level % 2
        return (
            pltpu.make_async_copy(chol_ref.at[level], low.at[p], load_sem.at[p]),
            pltpu.make_async_copy(noise_ref.at[level], draw.at[p], load_sem.at[2 + p]),
        )

    def load_factors(section):
        return pltpu.make_async_copy(fac_ref.at[section - 1], fac, load_sem.at[4])

    for copy in load_level(0):
        copy.start()

    barrier = pltpu.get_barrier_semaphore()

    def greet(device):
        pl.semaphore_signal(barrier, inc=1, device_id=device, device_id_type=MESH)

    for route in range(2):
        for d in FAR:
            greet({"lvl": across(route, d)})

    @pl.when(has_prior)
    def _():
        greet({"tile": tile - 1})
        for route in range(2):
            for d in FAR:
                greet({"tile": tile - 1, "lvl": across(route, d)})

    @pl.when(has_next)
    def _():
        greet({"tile": tile + 1})
        for route in range(2):
            for d in FAR:
                greet({"tile": tile + 1, "lvl": across(route, d)})

    def entry(section, n):
        number = parents[section - 1, n % NPAR, n // NPAR]
        clipped = jnp.maximum(number, 0)
        block = lax.rem(clipped, total_blocks)
        device = lax.div(block, blocks)
        local = lax.div(clipped, total_blocks) * blocks + lax.rem(block, blocks)
        return number >= 0, lax.div(device, peers) != tile, lax.rem(device, peers), local

    row = lax.broadcasted_iota(jnp.int32, (8, 128), 0)
    column = lax.broadcasted_iota(jnp.int32, (8, 128), 1)

    def ask(section):
        def one(n, carry):
            one_slot, two_slot, prior_slot = carry
            valid, prior, owner, local = entry(section, n)
            place = jnp.where(valid, jnp.where(prior, peers, 0) + owner, -1)
            here = (row == section - 1) & (column == place)
            there = (row == section - 1) & (column + peers == place) & (column < peers)
            here = here & (column < peers)
            two_slot = jnp.where(here & (one_slot >= 0), local, two_slot)
            one_slot = jnp.where(here & (one_slot < 0), local, one_slot)
            return one_slot, two_slot, jnp.where(there, local, prior_slot)

        return one

    state = (jnp.full((8, 128), -1, jnp.int32),) * 3
    for section in range(1, depth):
        state = lax.fori_loop(0, blocks * NPAR, ask(section), state)
    for slot in range(3):
        asked[slot] = jnp.maximum(state[slot], 0)

    ends = has_prior.astype(jnp.int32) + has_next.astype(jnp.int32)
    pl.semaphore_wait(barrier, 6 + 7 * ends)

    def peer(route, d):
        return 1 + 3 * route + FAR.index(d)

    def list_copies(which):
        moves = []
        if which == 1:
            moves.append((0, 0, {"tile": tile - 1}))
        for route in range(2):
            for d in FAR:
                device = {"lvl": across(route, d)}
                if which == 1:
                    device["tile"] = tile - 1
                moves.append((peer(route, d), peer(route, SIDE - d), device))
        return [
            remote(
                asked, lists.at[7 * which + theirs], list_s.at[7 * which + mine],
                list_r.at[7 * which + theirs], device,
            )
            for mine, theirs, device in moves
        ]

    for copy in list_copies(0):
        copy.start()

    @pl.when(has_prior)
    def _():
        for copy in list_copies(1):
            copy.start()

    WAYS = ((1, 1), (3, 3))

    def part(k):
        return pl.ds(k * piece, piece)

    def spread(level, chain, k):
        p = level % 2
        for route in range(2):
            own = held[level][chain][route]
            for way, (d, o) in enumerate(WAYS):
                remote(
                    own[0].at[part(k)], own[o].at[part(k)],
                    g1s.at[p, chain, route, way, k], g1r.at[p, chain, route, way, k],
                    {"lvl": along(route, d)},
                ).start()

    def forward(level, chain, start):
        p = level % 2
        for way, (d, o) in enumerate(WAYS):
            for route in range(2):
                own = held[level][chain][route]
                src = own[o].at[part(way)]
                if start:
                    arrived(src, g1r.at[p, chain, route, way, way])
                copy = remote(
                    src, own[2].at[part(way)], g2s.at[p, chain, route, way],
                    g2r.at[p, chain, route, way], {"lvl": along(route, d)},
                )
                if start:
                    copy.start()
                else:
                    copy.wait_send()

    def gathered(level, chain):
        p = level % 2
        for route in range(2):
            own = held[level][chain][route]
            for way, (d, o) in enumerate(WAYS):
                arrived(own[o].at[part(1 - way)], g1r.at[p, chain, route, way, 1 - way])
                arrived(own[2].at[part(way)], g2r.at[p, chain, route, way])

    def sent_on(level, chain):
        p = level % 2
        for route in range(2):
            own = held[level][chain][route]
            for way, (d, o) in enumerate(WAYS):
                for k in range(PIECES):
                    remote(
                        own[0].at[part(k)], own[0].at[part(k)],
                        g1s.at[p, chain, route, way, k], g1s.at[p, chain, route, way, k],
                        {"lvl": along(route, d)},
                    ).wait_send()
        forward(level, chain, False)

    def keep(level, chain, k, value):
        held[level][chain][0][0][k] = value[:tall]
        held[level][chain][1][0][k] = value[tall:]

    def product(level, k):
        p = level % 2
        return jnp.dot(low[p, k], draw[p, k], preferred_element_type=jnp.float32)

    for copy in load_level(0):
        copy.wait()
    for copy in load_level(1):
        copy.start()
    load_factors(1).start()

    def first(k, carry):
        value = product(0, k).astype(jnp.bfloat16)
        for chain in range(2):
            keep(0, chain, k, value[:, chain * wide : (chain + 1) * wide])
        return carry

    lax.fori_loop(0, piece, first, 0, unroll=4)
    spread(0, 0, 0)
    lax.fori_loop(piece, blocks, first, 0, unroll=4)
    for copy in load_level(2):
        copy.start()
    spread(0, 0, 1)
    for k in range(PIECES):
        spread(0, 1, k)

    def owner_lane(route, o):
        return at(-o, 0) if route == 0 else at(0, -o)

    def pick(section, chain, route, o, wanted):
        within = lax.rem(wanted, blocks)
        value = held[0][chain][route][o][within]
        for level in range(1, section):
            value = jnp.where(
                wanted >= level * blocks, held[level][chain][route][o][within], value
            )
        return value

    def build(section, chain, route):
        p = section % 2

        def one(i, carry):
            n = jnp.where(i == 3, 0, 1 + 3 * route + i)
            for o in range(SIDE):
                source = owner_lane(route, o)
                sent_next[chain][route][i * SIDE + o] = pick(
                    section, chain, route, o, table[7 + n, 2, section - 1, source]
                )
                for slot in range(CAP):
                    sent_same[chain][route][(i * SIDE + o) * CAP + slot] = pick(
                        section, chain, route, o, table[n, slot, section - 1, source]
                    )
            return carry

        lax.fori_loop(0, 3, one, 0)
        for o in range(SIDE):
            source = owner_lane(route, o)
            sent_next[chain][route][3 * SIDE + o] = pick(
                section, chain, route, o, table[7, 2, section - 1, source]
            )
            for slot in range(CAP):
                got[p][chain][route][o * CAP + slot] = pick(
                    section, chain, route, o, table[0, slot, section - 1, source]
                )

    def share(plane):
        return SIDE * (planes - 1 - plane) // planes

    def hand_next(section, chain, route, start):
        def act(copy):
            if start:
                copy.start()
            else:
                copy.wait_send()

        def direct(i, d, count):
            device = {"tile": tile + 1}
            if d:
                device["lvl"] = across(route, d)
            act(
                remote(
                    sent_next[chain][route].at[pl.ds(i * SIDE, count)],
                    cross[section - 1][chain][route].at[pl.ds(d * SIDE, count)],
                    cs.at[chain, route, d], cr.at[section - 1, chain, route, d], device,
                )
            )

        @pl.when(has_next & (tile % 2 == 0))
        def _():
            for i, d in enumerate(FAR + (0,)):
                direct(i, d, SIDE)

        for plane in range(planes - 1):

            @pl.when(tile == 2 * plane + 1)
            def _():
                count = share(plane)
                for i, d in enumerate(FAR):
                    place = pl.ds(i * SIDE + count, SIDE - count)
                    act(
                        remote(
                            sent_next[chain][route].at[place],
                            passed[section - 1][chain][route].at[place],
                            ps.at[chain, route, d], pr.at[section - 1, chain, route, d],
                            {"tile": tile + 1},
                        )
                    )
                for i, d in enumerate(FAR + (0,)):
                    direct(i, d, count if d else SIDE)

    def pass_next(section, chain, start):
        for plane in range(planes - 1):

            @pl.when(tile == 2 * plane + 2)
            def _():
                count = share(plane)
                for i, d in enumerate(FAR):
                    for route in range(2):
                        src = passed[section - 1][chain][route].at[
                            pl.ds(i * SIDE + count, SIDE - count)
                        ]
                        if start:
                            arrived(src, pr.at[section - 1, chain, route, d])
                        copy = remote(
                            src,
                            cross[section - 1][chain][route].at[
                                pl.ds(d * SIDE + count, SIDE - count)
                            ],
                            qs.at[chain, route, d], qr.at[section - 1, chain, route, d],
                            {"lvl": across(route, d)},
                        )
                        if start:
                            copy.start()
                        else:
                            copy.wait_send()

    def hand_same(section, chain, route, start, readers=FAR):
        p = section % 2
        size = SIDE * CAP
        for d in readers:
            i = FAR.index(d)
            copy = remote(
                sent_same[chain][route].at[pl.ds(i * size, size)],
                got[p][chain][route].at[pl.ds(d * size, size)],
                hs.at[chain, route, d], hr.at[p, chain, route, d],
                {"lvl": across(route, d)},
            )
            if start:
                copy.start()
            else:
                copy.wait_send()

    def received(section, chain):
        p = section % 2
        size = SIDE * CAP
        for route in range(2):
            for d in FAR:
                arrived(
                    got[p][chain][route].at[pl.ds(d * size, size)], hr.at[p, chain, route, d]
                )

        def prior(d, begin, count, sems):
            for route in range(2):
                arrived(
                    cross[section - 1][chain][route].at[pl.ds(d * SIDE + begin, count)],
                    sems.at[section - 1, chain, route, d],
                )

        @pl.when(tile % 2 == 1)
        def _():
            for d in range(SIDE):
                prior(d, 0, SIDE, cr)

        for plane in range(planes - 1):

            @pl.when(tile == 2 * plane + 2)
            def _():
                count = share(plane)
                prior(0, 0, SIDE, cr)
                for d in FAR:
                    prior(d, 0, count, cr)
                    prior(d, count, SIDE - count, qr)

    def output(level):
        return [
            pltpu.make_async_copy(
                held[level][chain][route][0],
                out_ref.at[level, :, pl.ds(route * tall, tall), pl.ds(chain * wide, wide)],
                out_sem.at[level, chain, route],
            )
            for chain in range(2)
            for route in range(2)
        ]

    def write_last(chain, k):
        columns = pl.ds(chain * wide, wide)
        return pltpu.make_async_copy(
            last.at[part(k), :, columns], out_ref.at[depth - 1, part(k), :, columns],
            out_sem.at[depth - 1, chain, k],
        )

    def mix(section, chain):
        p = section % 2

        def one(k, carry):
            total = base[k, :, chain * wide : (chain + 1) * wide]
            for slot in range(NPAR):
                code = codes[section - 1, k * NPAR + slot]
                kind = lax.div(code, 65536)
                halves = []
                for route in range(2):
                    place = lax.rem(code if route == 0 else lax.div(code, 256), 256)
                    same = got[p][chain][route][lax.rem(place, CAP * peers)]
                    prior = cross[section - 1][chain][route][lax.rem(lax.div(place, CAP), peers)]
                    value = jnp.where(kind == 2, prior, same)
                    halves.append(jnp.where(kind == 0, jnp.zeros_like(value), value))
                parent = jnp.concatenate(halves, axis=0)
                total = total + jnp.dot(
                    fac[k, slot], parent, preferred_element_type=jnp.float32
                )
            value = total.astype(jnp.bfloat16)
            if section < depth - 1:
                keep(section, chain, k, value)
            else:
                last[k, :, chain * wide : (chain + 1) * wide] = value
            return carry

        return one

    for section in range(1, depth):
        level = section - 1
        for chain in range(2):
            forward(level, chain, True)
        if section == 1:
            lists[0] = asked[...]
            for route in range(2):
                for d in FAR:
                    arrived(asked, list_r.at[peer(route, d)])

            @pl.when(has_next)
            def _():
                for n in range(7):
                    arrived(asked, list_r.at[7 + n])

            @pl.when(jnp.logical_not(has_next))
            def _():
                for n in range(7):
                    lists[7 + n] = asked[...]

            copy = pltpu.make_async_copy(lists, table, table_sem)
            copy.start()
            copy.wait()
        for chain in range(2):
            if section > 1:
                for route in range(2):
                    hand_next(section - 1, chain, route, False)
                    hand_same(section - 1, chain, route, False)
                pass_next(section - 1, chain, False)
            gathered(level, chain)
            for route in range(2):
                build(section, chain, route)
            for route in range(2):
                hand_next(section, chain, route, True)
            if chain == 0:
                for route in range(2):
                    hand_same(section, 0, route, True, FAR[:1])
        pass_next(section, 0, True)
        for route in range(2):
            hand_same(section, 0, route, True, FAR[1:])
        pass_next(section, 1, True)
        for route in range(2):
            hand_same(section, 1, route, True)

        if section == 1:

            def encode(n, carry):
                for s in range(1, depth):
                    valid, prior, owner, local = entry(s, n)
                    dx = lax.rem(ix - lax.div(owner, SIDE) + SIDE, SIDE)
                    dy = lax.rem(iy - lax.rem(owner, SIDE) + SIDE, SIDE)
                    slot = jnp.where(table[0, 0, s - 1, owner] == local, 0, 1)
                    near = (dy * SIDE + dx) * CAP + slot
                    turned = (dx * SIDE + dy) * CAP + slot
                    kind = jnp.where(valid, jnp.where(prior, 2, 1), 0)
                    codes[s - 1, n] = near + 256 * turned + 65536 * kind
                return carry

            lax.fori_loop(0, blocks * NPAR, encode, 0)

        for copy in load_level(section):
            copy.wait()

        def own(k, carry):
            base[k] = product(section, k)
            return carry

        lax.fori_loop(0, blocks, own, 0, unroll=4)
        if section + 2 < depth:
            for copy in load_level(section + 2):
                copy.start()
        for copy in output(level):
            copy.start()
        for chain in range(2):
            sent_on(level, chain)
        load_factors(section).wait()
        for chain in range(2):
            received(section, chain)
            for k in range(PIECES):
                lax.fori_loop(k * piece, (k + 1) * piece, mix(section, chain), 0, unroll=2)
                if section < depth - 1:
                    spread(section, chain, k)
                else:
                    write_last(chain, k).start()
        if section < depth - 1:
            load_factors(section + 1).start()

    for chain in range(2):
        for route in range(2):
            hand_next(depth - 1, chain, route, False)
            hand_same(depth - 1, chain, route, False)
        pass_next(depth - 1, chain, False)
    for copy in list_copies(0):
        copy.wait_send()

    @pl.when(has_prior)
    def _():
        for copy in list_copies(1):
            copy.wait_send()

    for level in range(depth - 1):
        for copy in output(level):
            copy.wait()
    for chain in range(2):
        for k in range(PIECES):
            write_last(chain, k).wait()


def settle(src, dst, hold, in_sem, out_sem):
    depth, blocks = src.shape[:2]
    parts = [
        (level, k, pl.ds(k * (blocks // PIECES), blocks // PIECES))
        for level in range(depth)
        for k in range(PIECES)
    ]
    for level, k, part in parts:
        pltpu.make_async_copy(
            src.at[level, part], hold.at[level, part], in_sem.at[level, k]
        ).start()
    for level, k, part in parts:
        pltpu.make_async_copy(
            src.at[level, part], hold.at[level, part], in_sem.at[level, k]
        ).wait()
        pltpu.make_async_copy(
            hold.at[level, part], dst.at[level, part], out_sem.at[level, k]
        ).start()
    for level, k, part in parts:
        pltpu.make_async_copy(
            hold.at[level, part], dst.at[level, part], out_sem.at[level, k]
        ).wait()


def shards(parents, factors, chol, noise):
    tiles = lax.axis_size("tile")
    depth, blocks, rows, _ = chol.shape
    real = noise.shape[3]
    peers = SIDE * SIDE

    def vmem(*shape, dtype=jnp.bfloat16):
        return pltpu.VMEM(shape, dtype)

    def half(count):
        return vmem(count, rows // 2, real // 2)

    def pairs(make):
        return [[make() for _ in range(2)] for _ in range(2)]

    dma = pltpu.SemaphoreType.DMA
    scratch = [
        [pairs(lambda: [half(blocks) for _ in range(SIDE)]) for _ in range(depth - 1)],
        [pairs(lambda: half(peers * CAP)) for _ in range(2)],
        [pairs(lambda: half(peers)) for _ in range(depth - 1)],
        [pairs(lambda: half(3 * SIDE)) for _ in range(depth - 1)],
        pairs(lambda: half(3 * SIDE * CAP)),
        pairs(lambda: half(4 * SIDE)),
        vmem(blocks, NPAR, rows, rows),
        vmem(2, blocks, rows, rows),
        vmem(2, blocks, rows, real),
        vmem(blocks, rows, real, dtype=jnp.float32),
        vmem(blocks, rows, real),
        vmem(3, 8, 128, dtype=jnp.int32),
        vmem(14, 3, 8, 128, dtype=jnp.int32),
        pltpu.SMEM((14, 3, 8, 128), jnp.int32),
        pltpu.SMEM((depth - 1, blocks * NPAR), jnp.int32),
        dma((2, 2, 2, 2, PIECES)), dma((2, 2, 2, 2, PIECES)),
        dma((2, 2, 2, 2)), dma((2, 2, 2, 2)),
        dma((2, 2, SIDE)), dma((2, 2, 2, SIDE)),
        dma((2, 2, SIDE)), dma((depth - 1, 2, 2, SIDE)),
        dma((2, 2, SIDE)), dma((depth - 1, 2, 2, SIDE)),
        dma((2, 2, SIDE)), dma((depth - 1, 2, 2, SIDE)),
        dma((14,)), dma((14,)),
        dma((5,)), dma((depth, 2, 2)), dma,
    ]
    flat, tree = jax.tree.flatten(scratch)

    def body(*refs):
        operands, rest = refs[:5], refs[5:]
        kernel(
            (depth, blocks, rows, real, tiles), *operands, *jax.tree.unflatten(tree, rest)
        )

    anywhere = pl.BlockSpec(memory_space=pl.ANY)
    field = pl.pallas_call(
        body,
        out_shape=jax.ShapeDtypeStruct((depth, blocks, rows, real), jnp.bfloat16),
        in_specs=[pl.BlockSpec(memory_space=pltpu.SMEM), anywhere, anywhere, anywhere],
        out_specs=anywhere,
        scratch_shapes=flat,
        compiler_params=pltpu.CompilerParams(
            collective_id=0, has_side_effects=True, vmem_limit_bytes=67043328
        ),
        name="field",
    )(parents.transpose(0, 2, 1), factors, chol, noise)
    return pl.pallas_call(
        settle,
        out_shape=jax.ShapeDtypeStruct(field.shape, field.dtype),
        in_specs=[anywhere],
        out_specs=anywhere,
        scratch_shapes=[
            vmem(*field.shape), dma((depth, PIECES)), dma((depth, PIECES)),
        ],
        name="settle",
    )(field)


def solution(mesh):
    placed = (
        P(None, ("tile", "lvl"), None),
        P(None, ("tile", "lvl"), None, None, None),
        P(None, ("tile", "lvl"), None, None),
        P(None, ("tile", "lvl"), None, None),
    )
    return jax.shard_map(
        shards,
        mesh=mesh,
        in_specs=placed,
        out_specs=P(None, ("tile", "lvl"), None, None),
        check_vma=False,
    )
```

```python
import jax
import jax.numpy as jnp
from jax import lax
from jax.experimental import pallas as pl
from jax.experimental.pallas import tpu as pltpu
from jax.sharding import PartitionSpec as P

MESH = pl.DeviceIdType.MESH
NPAR = 4
CAP = 2
SIDE = 4
FAR = (2, 1, 3)
PIECES = 2


def kernel(
    dims, parents, fac_ref, chol_ref, noise_ref, out_ref,
    held, got, cross, passed, sent_same, sent_next, fac, low, draw, base, last,
    asked, lists, table, codes, g1s, g1r, g2s, g2r, hs, hr, cs, cr, ps, pr, qs, qr,
    list_s, list_r, load_sem, out_sem, table_sem,
):
    depth, blocks, rows, real, tiles = dims
    tall, wide = rows // 2, real // 2
    piece = blocks // PIECES
    peers = SIDE * SIDE
    planes = tiles // 2
    total_blocks = blocks * peers * tiles
    tile = lax.axis_index("tile")
    lane = lax.axis_index("lvl")
    ix, iy = lane // SIDE, lane % SIDE
    has_prior = tile > 0
    has_next = tile < tiles - 1

    def at(dx, dy):
        return ((ix + dx) % SIDE) * SIDE + (iy + dy) % SIDE

    def along(route, d):
        return at(d, 0) if route == 0 else at(0, d)

    def across(route, d):
        return along(1 - route, d)

    def remote(src, dst, ssem, rsem, device):
        return pltpu.make_async_remote_copy(
            src_ref=src, dst_ref=dst, send_sem=ssem, recv_sem=rsem,
            device_id=device, device_id_type=MESH,
        )

    def arrived(ref, sem):
        remote(ref, ref, sem, sem, {"lvl": at(1, 0)}).wait_recv()

    def load_level(level):
        p = level % 2
        return (
            pltpu.make_async_copy(chol_ref.at[level], low.at[p], load_sem.at[p]),
            pltpu.make_async_copy(noise_ref.at[level], draw.at[p], load_sem.at[2 + p]),
        )

    def load_factors(section):
        return pltpu.make_async_copy(fac_ref.at[section - 1], fac, load_sem.at[4])

    for copy in load_level(0):
        copy.start()

    barrier = pltpu.get_barrier_semaphore()

    def greet(device):
        pl.semaphore_signal(barrier, inc=1, device_id=device, device_id_type=MESH)

    for route in range(2):
        for d in FAR:
            greet({"lvl": across(route, d)})

    @pl.when(has_prior)
    def _():
        greet({"tile": tile - 1})
        for route in range(2):
            for d in FAR:
                greet({"tile": tile - 1, "lvl": across(route, d)})

    @pl.when(has_next)
    def _():
        greet({"tile": tile + 1})
        for route in range(2):
            for d in FAR:
                greet({"tile": tile + 1, "lvl": across(route, d)})

    odd = tile % 2 == 1
    skips_back, skips_on = odd & (tile > 1), odd & (tile < tiles - 1)

    @pl.when(skips_back)
    def _():
        greet({"tile": tile - 2})

    @pl.when(skips_on)
    def _():
        greet({"tile": tile + 2})

    def entry(section, n):
        number = parents[section - 1, n % NPAR, n // NPAR]
        clipped = jnp.maximum(number, 0)
        block = lax.rem(clipped, total_blocks)
        device = lax.div(block, blocks)
        local = lax.div(clipped, total_blocks) * blocks + lax.rem(block, blocks)
        return number >= 0, lax.div(device, peers) != tile, lax.rem(device, peers), local

    row = lax.broadcasted_iota(jnp.int32, (8, 128), 0)
    column = lax.broadcasted_iota(jnp.int32, (8, 128), 1)

    def ask(section):
        def one(n, carry):
            one_slot, two_slot, prior_slot = carry
            valid, prior, owner, local = entry(section, n)
            place = jnp.where(valid, jnp.where(prior, peers, 0) + owner, -1)
            here = (row == section - 1) & (column == place)
            there = (row == section - 1) & (column + peers == place) & (column < peers)
            here = here & (column < peers)
            two_slot = jnp.where(here & (one_slot >= 0), local, two_slot)
            one_slot = jnp.where(here & (one_slot < 0), local, one_slot)
            return one_slot, two_slot, jnp.where(there, local, prior_slot)

        return one

    state = (jnp.full((8, 128), -1, jnp.int32),) * 3
    for section in range(1, depth):
        state = lax.fori_loop(0, blocks * NPAR, ask(section), state)
    for slot in range(3):
        asked[slot] = jnp.maximum(state[slot], 0)

    ends = has_prior.astype(jnp.int32) + has_next.astype(jnp.int32)
    skips = skips_back.astype(jnp.int32) + skips_on.astype(jnp.int32)
    pl.semaphore_wait(barrier, 6 + 7 * ends + skips)

    def peer(route, d):
        return 1 + 3 * route + FAR.index(d)

    def list_copies(which):
        moves = []
        if which == 1:
            moves.append((0, 0, {"tile": tile - 1}))
        for route in range(2):
            for d in FAR:
                device = {"lvl": across(route, d)}
                if which == 1:
                    device["tile"] = tile - 1
                moves.append((peer(route, d), peer(route, SIDE - d), device))
        return [
            remote(
                asked, lists.at[7 * which + theirs], list_s.at[7 * which + mine],
                list_r.at[7 * which + theirs], device,
            )
            for mine, theirs, device in moves
        ]

    for copy in list_copies(0):
        copy.start()

    @pl.when(has_prior)
    def _():
        for copy in list_copies(1):
            copy.start()

    WAYS = ((1, 1), (3, 3))

    def part(k):
        return pl.ds(k * piece, piece)

    def spread(level, chain, k):
        p = level % 2
        for route in range(2):
            own = held[level][chain][route]
            for way, (d, o) in enumerate(WAYS):
                remote(
                    own[0].at[part(k)], own[o].at[part(k)],
                    g1s.at[p, chain, route, way, k], g1r.at[p, chain, route, way, k],
                    {"lvl": along(route, d)},
                ).start()

    def forward(level, chain, start):
        p = level % 2
        for way, (d, o) in enumerate(WAYS):
            for route in range(2):
                own = held[level][chain][route]
                src = own[o].at[part(way)]
                if start:
                    arrived(src, g1r.at[p, chain, route, way, way])
                copy = remote(
                    src, own[2].at[part(way)], g2s.at[p, chain, route, way],
                    g2r.at[p, chain, route, way], {"lvl": along(route, d)},
                )
                if start:
                    copy.start()
                else:
                    copy.wait_send()

    def gathered(level, chain):
        p = level % 2
        for route in range(2):
            own = held[level][chain][route]
            for way, (d, o) in enumerate(WAYS):
                arrived(own[o].at[part(1 - way)], g1r.at[p, chain, route, way, 1 - way])
                arrived(own[2].at[part(way)], g2r.at[p, chain, route, way])

    def sent_on(level, chain):
        p = level % 2
        for route in range(2):
            own = held[level][chain][route]
            for way, (d, o) in enumerate(WAYS):
                for k in range(PIECES):
                    remote(
                        own[0].at[part(k)], own[0].at[part(k)],
                        g1s.at[p, chain, route, way, k], g1s.at[p, chain, route, way, k],
                        {"lvl": along(route, d)},
                    ).wait_send()
        forward(level, chain, False)

    def keep(level, chain, k, value):
        held[level][chain][0][0][k] = value[:tall]
        held[level][chain][1][0][k] = value[tall:]

    def product(level, k):
        p = level % 2
        return jnp.dot(low[p, k], draw[p, k], preferred_element_type=jnp.float32)

    for copy in load_level(0):
        copy.wait()
    for copy in load_level(1):
        copy.start()
    load_factors(1).start()

    def first(k, carry):
        value = product(0, k).astype(jnp.bfloat16)
        for chain in range(2):
            keep(0, chain, k, value[:, chain * wide : (chain + 1) * wide])
        return carry

    lax.fori_loop(0, piece, first, 0, unroll=4)
    spread(0, 0, 0)
    lax.fori_loop(piece, blocks, first, 0, unroll=4)
    for copy in load_level(2):
        copy.start()
    spread(0, 0, 1)
    for k in range(PIECES):
        spread(0, 1, k)

    def owner_lane(route, o):
        return at(-o, 0) if route == 0 else at(0, -o)

    def pick(section, chain, route, o, wanted):
        within = lax.rem(wanted, blocks)
        value = held[0][chain][route][o][within]
        for level in range(1, section):
            value = jnp.where(
                wanted >= level * blocks, held[level][chain][route][o][within], value
            )
        return value

    def build(section, chain, route):
        p = section % 2

        def one(i, carry):
            n = jnp.where(i == 3, 0, 1 + 3 * route + i)
            for o in range(SIDE):
                source = owner_lane(route, o)
                sent_next[chain][route][i * SIDE + o] = pick(
                    section, chain, route, o, table[7 + n, 2, section - 1, source]
                )
                for slot in range(CAP):
                    sent_same[chain][route][(i * SIDE + o) * CAP + slot] = pick(
                        section, chain, route, o, table[n, slot, section - 1, source]
                    )
            return carry

        lax.fori_loop(0, 3, one, 0)
        for o in range(SIDE):
            source = owner_lane(route, o)
            sent_next[chain][route][3 * SIDE + o] = pick(
                section, chain, route, o, table[7, 2, section - 1, source]
            )
            for slot in range(CAP):
                got[p][chain][route][o * CAP + slot] = pick(
                    section, chain, route, o, table[0, slot, section - 1, source]
                )

    def share(plane, section):
        count = SIDE * (planes - 1 - plane) // planes
        return count - 1 if section == depth - 1 and count > 1 else count

    def hand_next(section, chain, route, start):
        def act(copy):
            if start:
                copy.start()
            else:
                copy.wait_send()

        def direct(i, d, count):
            device = {"tile": tile + 1}
            if d:
                device["lvl"] = across(route, d)
            act(
                remote(
                    sent_next[chain][route].at[pl.ds(i * SIDE, count)],
                    cross[section - 1][chain][route].at[pl.ds(d * SIDE, count)],
                    cs.at[chain, route, d], cr.at[section - 1, chain, route, d], device,
                )
            )

        @pl.when(has_next & (tile % 2 == 0))
        def _():
            for i, d in enumerate(FAR + (0,)):
                direct(i, d, SIDE)

        for plane in range(planes - 1):

            @pl.when(tile == 2 * plane + 1)
            def _():
                count = share(plane, section)
                for i, d in enumerate(FAR):
                    place = pl.ds(i * SIDE + count, SIDE - count)
                    act(
                        remote(
                            sent_next[chain][route].at[place],
                            passed[section - 1][chain][route].at[place],
                            ps.at[chain, route, d], pr.at[section - 1, chain, route, d],
                            {"tile": tile + 2},
                        )
                    )
                for i, d in enumerate(FAR + (0,)):
                    direct(i, d, count if d else SIDE)

    def pass_next(section, chain, start):
        for plane in range(planes - 1):

            @pl.when(tile == 2 * plane + 3)
            def _():
                count = share(plane, section)
                for i, d in enumerate(FAR):
                    for route in range(2):
                        src = passed[section - 1][chain][route].at[
                            pl.ds(i * SIDE + count, SIDE - count)
                        ]
                        if start:
                            arrived(src, pr.at[section - 1, chain, route, d])
                        copy = remote(
                            src,
                            cross[section - 1][chain][route].at[
                                pl.ds(d * SIDE + count, SIDE - count)
                            ],
                            qs.at[chain, route, d], qr.at[section - 1, chain, route, d],
                            {"tile": tile - 1, "lvl": across(route, d)},
                        )
                        if start:
                            copy.start()
                        else:
                            copy.wait_send()

    def hand_same(section, chain, route, start, readers=FAR):
        p = section % 2
        size = SIDE * CAP
        for d in readers:
            i = FAR.index(d)
            copy = remote(
                sent_same[chain][route].at[pl.ds(i * size, size)],
                got[p][chain][route].at[pl.ds(d * size, size)],
                hs.at[chain, route, d], hr.at[p, chain, route, d],
                {"lvl": across(route, d)},
            )
            if start:
                copy.start()
            else:
                copy.wait_send()

    def received(section, chain):
        p = section % 2
        size = SIDE * CAP
        for route in range(2):
            for d in FAR:
                arrived(
                    got[p][chain][route].at[pl.ds(d * size, size)], hr.at[p, chain, route, d]
                )

        def prior(d, begin, count, sems):
            for route in range(2):
                arrived(
                    cross[section - 1][chain][route].at[pl.ds(d * SIDE + begin, count)],
                    sems.at[section - 1, chain, route, d],
                )

        @pl.when(tile % 2 == 1)
        def _():
            for d in range(SIDE):
                prior(d, 0, SIDE, cr)

        for plane in range(planes - 1):

            @pl.when(tile == 2 * plane + 2)
            def _():
                count = share(plane, section)
                prior(0, 0, SIDE, cr)
                for d in FAR:
                    prior(d, 0, count, cr)
                    prior(d, count, SIDE - count, qr)

    def output(level):
        return [
            pltpu.make_async_copy(
                held[level][chain][route][0],
                out_ref.at[level, :, pl.ds(route * tall, tall), pl.ds(chain * wide, wide)],
                out_sem.at[level, chain, route],
            )
            for chain in range(2)
            for route in range(2)
        ]

    def write_last(chain, k):
        columns = pl.ds(chain * wide, wide)
        return pltpu.make_async_copy(
            last.at[part(k), :, columns], out_ref.at[depth - 1, part(k), :, columns],
            out_sem.at[depth - 1, chain, k],
        )

    def mix(section, chain):
        p = section % 2

        def one(k, carry):
            total = base[k, :, chain * wide : (chain + 1) * wide]
            for slot in range(NPAR):
                code = codes[section - 1, k * NPAR + slot]
                kind = lax.div(code, 65536)
                halves = []
                for route in range(2):
                    place = lax.rem(code if route == 0 else lax.div(code, 256), 256)
                    same = got[p][chain][route][lax.rem(place, CAP * peers)]
                    prior = cross[section - 1][chain][route][lax.rem(lax.div(place, CAP), peers)]
                    value = jnp.where(kind == 2, prior, same)
                    halves.append(jnp.where(kind == 0, jnp.zeros_like(value), value))
                parent = jnp.concatenate(halves, axis=0)
                total = total + jnp.dot(
                    fac[k, slot], parent, preferred_element_type=jnp.float32
                )
            value = total.astype(jnp.bfloat16)
            if section < depth - 1:
                keep(section, chain, k, value)
            else:
                last[k, :, chain * wide : (chain + 1) * wide] = value
            return carry

        return one

    for section in range(1, depth):
        level = section - 1
        for chain in range(2):
            forward(level, chain, True)
        if section == 1:
            lists[0] = asked[...]
            for route in range(2):
                for d in FAR:
                    arrived(asked, list_r.at[peer(route, d)])

            @pl.when(has_next)
            def _():
                for n in range(7):
                    arrived(asked, list_r.at[7 + n])

            @pl.when(jnp.logical_not(has_next))
            def _():
                for n in range(7):
                    lists[7 + n] = asked[...]

            copy = pltpu.make_async_copy(lists, table, table_sem)
            copy.start()
            copy.wait()
        for chain in range(2):
            if section > 1:
                for route in range(2):
                    hand_next(section - 1, chain, route, False)
                    hand_same(section - 1, chain, route, False)
                pass_next(section - 1, chain, False)
            gathered(level, chain)
            for route in range(2):
                build(section, chain, route)
            for route in range(2):
                hand_next(section, chain, route, True)
            if chain == 0:
                for route in range(2):
                    hand_same(section, 0, route, True, FAR[:1])
        pass_next(section, 0, True)
        for route in range(2):
            hand_same(section, 0, route, True, FAR[1:])
        pass_next(section, 1, True)
        for route in range(2):
            hand_same(section, 1, route, True)

        if section == 1:

            def encode(n, carry):
                for s in range(1, depth):
                    valid, prior, owner, local = entry(s, n)
                    dx = lax.rem(ix - lax.div(owner, SIDE) + SIDE, SIDE)
                    dy = lax.rem(iy - lax.rem(owner, SIDE) + SIDE, SIDE)
                    slot = jnp.where(table[0, 0, s - 1, owner] == local, 0, 1)
                    near = (dy * SIDE + dx) * CAP + slot
                    turned = (dx * SIDE + dy) * CAP + slot
                    kind = jnp.where(valid, jnp.where(prior, 2, 1), 0)
                    codes[s - 1, n] = near + 256 * turned + 65536 * kind
                return carry

            lax.fori_loop(0, blocks * NPAR, encode, 0)

        for copy in load_level(section):
            copy.wait()

        def own(k, carry):
            base[k] = product(section, k)
            return carry

        lax.fori_loop(0, blocks, own, 0, unroll=4)
        if section + 2 < depth:
            for copy in load_level(section + 2):
                copy.start()
        for copy in output(level):
            copy.start()
        for chain in range(2):
            sent_on(level, chain)
        load_factors(section).wait()
        for chain in range(2):
            received(section, chain)
            for k in range(PIECES):
                lax.fori_loop(k * piece, (k + 1) * piece, mix(section, chain), 0, unroll=2)
                if section < depth - 1:
                    spread(section, chain, k)
                else:
                    write_last(chain, k).start()
        if section < depth - 1:
            load_factors(section + 1).start()

    for chain in range(2):
        for route in range(2):
            hand_next(depth - 1, chain, route, False)
            hand_same(depth - 1, chain, route, False)
        pass_next(depth - 1, chain, False)
    for copy in list_copies(0):
        copy.wait_send()

    @pl.when(has_prior)
    def _():
        for copy in list_copies(1):
            copy.wait_send()

    for level in range(depth - 1):
        for copy in output(level):
            copy.wait()
    for chain in range(2):
        for k in range(PIECES):
            write_last(chain, k).wait()


def settle(src, dst, hold, in_sem, out_sem):
    depth, blocks = src.shape[:2]
    parts = [
        (level, k, pl.ds(k * (blocks // PIECES), blocks // PIECES))
        for level in range(depth)
        for k in range(PIECES)
    ]
    for level, k, part in parts:
        pltpu.make_async_copy(
            src.at[level, part], hold.at[level, part], in_sem.at[level, k]
        ).start()
    for level, k, part in parts:
        pltpu.make_async_copy(
            src.at[level, part], hold.at[level, part], in_sem.at[level, k]
        ).wait()
        pltpu.make_async_copy(
            hold.at[level, part], dst.at[level, part], out_sem.at[level, k]
        ).start()
    for level, k, part in parts:
        pltpu.make_async_copy(
            hold.at[level, part], dst.at[level, part], out_sem.at[level, k]
        ).wait()


def shards(parents, factors, chol, noise):
    tiles = lax.axis_size("tile")
    depth, blocks, rows, _ = chol.shape
    real = noise.shape[3]
    peers = SIDE * SIDE

    def vmem(*shape, dtype=jnp.bfloat16):
        return pltpu.VMEM(shape, dtype)

    def half(count):
        return vmem(count, rows // 2, real // 2)

    def pairs(make):
        return [[make() for _ in range(2)] for _ in range(2)]

    dma = pltpu.SemaphoreType.DMA
    scratch = [
        [pairs(lambda: [half(blocks) for _ in range(SIDE)]) for _ in range(depth - 1)],
        [pairs(lambda: half(peers * CAP)) for _ in range(2)],
        [pairs(lambda: half(peers)) for _ in range(depth - 1)],
        [pairs(lambda: half(3 * SIDE)) for _ in range(depth - 1)],
        pairs(lambda: half(3 * SIDE * CAP)),
        pairs(lambda: half(4 * SIDE)),
        vmem(blocks, NPAR, rows, rows),
        vmem(2, blocks, rows, rows),
        vmem(2, blocks, rows, real),
        vmem(blocks, rows, real, dtype=jnp.float32),
        vmem(blocks, rows, real),
        vmem(3, 8, 128, dtype=jnp.int32),
        vmem(14, 3, 8, 128, dtype=jnp.int32),
        pltpu.SMEM((14, 3, 8, 128), jnp.int32),
        pltpu.SMEM((depth - 1, blocks * NPAR), jnp.int32),
        dma((2, 2, 2, 2, PIECES)), dma((2, 2, 2, 2, PIECES)),
        dma((2, 2, 2, 2)), dma((2, 2, 2, 2)),
        dma((2, 2, SIDE)), dma((2, 2, 2, SIDE)),
        dma((2, 2, SIDE)), dma((depth - 1, 2, 2, SIDE)),
        dma((2, 2, SIDE)), dma((depth - 1, 2, 2, SIDE)),
        dma((2, 2, SIDE)), dma((depth - 1, 2, 2, SIDE)),
        dma((14,)), dma((14,)),
        dma((5,)), dma((depth, 2, 2)), dma,
    ]
    flat, tree = jax.tree.flatten(scratch)

    def body(*refs):
        operands, rest = refs[:5], refs[5:]
        kernel(
            (depth, blocks, rows, real, tiles), *operands, *jax.tree.unflatten(tree, rest)
        )

    anywhere = pl.BlockSpec(memory_space=pl.ANY)
    field = pl.pallas_call(
        body,
        out_shape=jax.ShapeDtypeStruct((depth, blocks, rows, real), jnp.bfloat16),
        in_specs=[pl.BlockSpec(memory_space=pltpu.SMEM), anywhere, anywhere, anywhere],
        out_specs=anywhere,
        scratch_shapes=flat,
        compiler_params=pltpu.CompilerParams(
            collective_id=0, has_side_effects=True, vmem_limit_bytes=67043328
        ),
        name="field",
    )(parents.transpose(0, 2, 1), factors, chol, noise)
    return pl.pallas_call(
        settle,
        out_shape=jax.ShapeDtypeStruct(field.shape, field.dtype),
        in_specs=[anywhere],
        out_specs=anywhere,
        scratch_shapes=[
            vmem(*field.shape), dma((depth, PIECES)), dma((depth, PIECES)),
        ],
        name="settle",
    )(field)


def solution(mesh):
    placed = (
        P(None, ("tile", "lvl"), None),
        P(None, ("tile", "lvl"), None, None, None),
        P(None, ("tile", "lvl"), None, None),
        P(None, ("tile", "lvl"), None, None),
    )
    return jax.shard_map(
        shards,
        mesh=mesh,
        in_specs=placed,
        out_specs=P(None, ("tile", "lvl"), None, None),
        check_vma=False,
    )
```

```python
import jax
import jax.numpy as jnp
from jax import lax
from jax.experimental import pallas as pl
from jax.experimental.pallas import tpu as pltpu
from jax.sharding import PartitionSpec as P

MESH = pl.DeviceIdType.MESH
NPAR = 4
CAP = 2
SIDE = 4
FAR = (2, 1, 3)
PIECES = 2


def kernel(
    dims, parents, fac_ref, chol_ref, noise_ref, out_ref,
    held, got, cross, passed, sent_same, sent_next, fac, low, draw, base, last,
    asked, lists, table, codes, g1s, g1r, g2s, g2r, hs, hr, cs, cr, ps, pr, qs, qr,
    list_s, list_r, load_sem, out_sem, table_sem,
):
    depth, blocks, rows, real, tiles = dims
    tall, wide = rows // 2, real // 2
    piece = blocks // PIECES
    peers = SIDE * SIDE
    planes = tiles // 2
    total_blocks = blocks * peers * tiles
    tile = lax.axis_index("tile")
    lane = lax.axis_index("lvl")
    ix, iy = lane // SIDE, lane % SIDE
    has_prior = tile > 0
    has_next = tile < tiles - 1

    def at(dx, dy):
        return ((ix + dx) % SIDE) * SIDE + (iy + dy) % SIDE

    def along(route, d):
        return at(d, 0) if route == 0 else at(0, d)

    def across(route, d):
        return along(1 - route, d)

    def remote(src, dst, ssem, rsem, device):
        return pltpu.make_async_remote_copy(
            src_ref=src, dst_ref=dst, send_sem=ssem, recv_sem=rsem,
            device_id=device, device_id_type=MESH,
        )

    def arrived(ref, sem):
        remote(ref, ref, sem, sem, {"lvl": at(1, 0)}).wait_recv()

    def load_level(level):
        p = level % 2
        return (
            pltpu.make_async_copy(chol_ref.at[level], low.at[p], load_sem.at[p]),
            pltpu.make_async_copy(noise_ref.at[level], draw.at[p], load_sem.at[2 + p]),
        )

    def load_factors(section):
        return pltpu.make_async_copy(fac_ref.at[section - 1], fac, load_sem.at[4])

    for copy in load_level(0):
        copy.start()

    barrier = pltpu.get_barrier_semaphore()

    def greet(device):
        pl.semaphore_signal(barrier, inc=1, device_id=device, device_id_type=MESH)

    for route in range(2):
        for d in FAR:
            greet({"lvl": across(route, d)})

    @pl.when(has_prior)
    def _():
        greet({"tile": tile - 1})
        for route in range(2):
            for d in FAR:
                greet({"tile": tile - 1, "lvl": across(route, d)})

    @pl.when(has_next)
    def _():
        greet({"tile": tile + 1})
        for route in range(2):
            for d in FAR:
                greet({"tile": tile + 1, "lvl": across(route, d)})

    odd = tile % 2 == 1
    skips_back, skips_on = odd & (tile > 1), odd & (tile < tiles - 1)

    @pl.when(skips_back)
    def _():
        greet({"tile": tile - 2})

    @pl.when(skips_on)
    def _():
        greet({"tile": tile + 2})

    def entry(section, n):
        number = parents[section - 1, n % NPAR, n // NPAR]
        clipped = jnp.maximum(number, 0)
        block = lax.rem(clipped, total_blocks)
        device = lax.div(block, blocks)
        local = lax.div(clipped, total_blocks) * blocks + lax.rem(block, blocks)
        return number >= 0, lax.div(device, peers) != tile, lax.rem(device, peers), local

    row = lax.broadcasted_iota(jnp.int32, (8, 128), 0)
    column = lax.broadcasted_iota(jnp.int32, (8, 128), 1)

    def ask(section):
        def one(n, carry):
            one_slot, two_slot, prior_slot = carry
            valid, prior, owner, local = entry(section, n)
            place = jnp.where(valid, jnp.where(prior, peers, 0) + owner, -1)
            here = (row == section - 1) & (column == place)
            there = (row == section - 1) & (column + peers == place) & (column < peers)
            here = here & (column < peers)
            two_slot = jnp.where(here & (one_slot >= 0), local, two_slot)
            one_slot = jnp.where(here & (one_slot < 0), local, one_slot)
            return one_slot, two_slot, jnp.where(there, local, prior_slot)

        return one

    state = (jnp.full((8, 128), -1, jnp.int32),) * 3
    for section in range(1, depth):
        state = lax.fori_loop(0, blocks * NPAR, ask(section), state)
    for slot in range(3):
        asked[slot] = jnp.maximum(state[slot], 0)

    ends = has_prior.astype(jnp.int32) + has_next.astype(jnp.int32)
    skips = skips_back.astype(jnp.int32) + skips_on.astype(jnp.int32)
    pl.semaphore_wait(barrier, 6 + 7 * ends + skips)

    def peer(route, d):
        return 1 + 3 * route + FAR.index(d)

    def list_copies(which):
        moves = []
        if which == 1:
            moves.append((0, 0, {"tile": tile - 1}))
        for route in range(2):
            for d in FAR:
                device = {"lvl": across(route, d)}
                if which == 1:
                    device["tile"] = tile - 1
                moves.append((peer(route, d), peer(route, SIDE - d), device))
        return [
            remote(
                asked, lists.at[7 * which + theirs], list_s.at[7 * which + mine],
                list_r.at[7 * which + theirs], device,
            )
            for mine, theirs, device in moves
        ]

    for copy in list_copies(0):
        copy.start()

    @pl.when(has_prior)
    def _():
        for copy in list_copies(1):
            copy.start()

    WAYS = ((1, 1), (3, 3))

    def part(k):
        return pl.ds(k * piece, piece)

    def spread(level, chain, k):
        p = level % 2
        for route in range(2):
            own = held[level][chain][route]
            for way, (d, o) in enumerate(WAYS):
                remote(
                    own[0].at[part(k)], own[o].at[part(k)],
                    g1s.at[p, chain, route, way, k], g1r.at[p, chain, route, way, k],
                    {"lvl": along(route, d)},
                ).start()

    def forward(level, chain, start):
        p = level % 2
        for way, (d, o) in enumerate(WAYS):
            for route in range(2):
                own = held[level][chain][route]
                src = own[o].at[part(way)]
                if start:
                    arrived(src, g1r.at[p, chain, route, way, way])
                copy = remote(
                    src, own[2].at[part(way)], g2s.at[p, chain, route, way],
                    g2r.at[p, chain, route, way], {"lvl": along(route, d)},
                )
                if start:
                    copy.start()
                else:
                    copy.wait_send()

    def gathered(level, chain):
        p = level % 2
        for route in range(2):
            own = held[level][chain][route]
            for way, (d, o) in enumerate(WAYS):
                arrived(own[o].at[part(1 - way)], g1r.at[p, chain, route, way, 1 - way])
                arrived(own[2].at[part(way)], g2r.at[p, chain, route, way])

    def sent_on(level, chain):
        p = level % 2
        for route in range(2):
            own = held[level][chain][route]
            for way, (d, o) in enumerate(WAYS):
                for k in range(PIECES):
                    remote(
                        own[0].at[part(k)], own[0].at[part(k)],
                        g1s.at[p, chain, route, way, k], g1s.at[p, chain, route, way, k],
                        {"lvl": along(route, d)},
                    ).wait_send()
        forward(level, chain, False)

    def keep(level, chain, k, value):
        held[level][chain][0][0][k] = value[:tall]
        held[level][chain][1][0][k] = value[tall:]

    def product(level, k):
        p = level % 2
        return jnp.dot(low[p, k], draw[p, k], preferred_element_type=jnp.float32)

    for copy in load_level(0):
        copy.wait()
    for copy in load_level(1):
        copy.start()
    load_factors(1).start()

    def first(k, carry):
        value = product(0, k).astype(jnp.bfloat16)
        for chain in range(2):
            keep(0, chain, k, value[:, chain * wide : (chain + 1) * wide])
        return carry

    lax.fori_loop(0, piece, first, 0, unroll=4)
    spread(0, 0, 0)
    lax.fori_loop(piece, blocks, first, 0, unroll=4)
    for copy in load_level(2):
        copy.start()
    spread(0, 0, 1)
    for k in range(PIECES):
        spread(0, 1, k)

    def owner_lane(route, o):
        return at(-o, 0) if route == 0 else at(0, -o)

    def pick(section, chain, route, o, wanted):
        within = lax.rem(wanted, blocks)
        value = held[0][chain][route][o][within]
        for level in range(1, section):
            value = jnp.where(
                wanted >= level * blocks, held[level][chain][route][o][within], value
            )
        return value

    def build(section, chain, route):
        p = section % 2

        def one(i, carry):
            n = jnp.where(i == 3, 0, 1 + 3 * route + i)
            for o in range(SIDE):
                source = owner_lane(route, o)
                sent_next[chain][route][i * SIDE + o] = pick(
                    section, chain, route, o, table[7 + n, 2, section - 1, source]
                )
                for slot in range(CAP):
                    sent_same[chain][route][(i * SIDE + o) * CAP + slot] = pick(
                        section, chain, route, o, table[n, slot, section - 1, source]
                    )
            return carry

        lax.fori_loop(0, 3, one, 0)
        for o in range(SIDE):
            source = owner_lane(route, o)
            sent_next[chain][route][3 * SIDE + o] = pick(
                section, chain, route, o, table[7, 2, section - 1, source]
            )
            for slot in range(CAP):
                got[p][chain][route][o * CAP + slot] = pick(
                    section, chain, route, o, table[0, slot, section - 1, source]
                )

    def share(plane, section):
        count = SIDE * (planes - 1 - plane) // planes
        return count - 1 if section == depth - 1 and count > 1 else count

    def hand_next(section, chain, route, start):
        def act(copy):
            if start:
                copy.start()
            else:
                copy.wait_send()

        def direct(i, d, count):
            device = {"tile": tile + 1}
            if d:
                device["lvl"] = across(route, d)
            act(
                remote(
                    sent_next[chain][route].at[pl.ds(i * SIDE, count)],
                    cross[section - 1][chain][route].at[pl.ds(d * SIDE, count)],
                    cs.at[chain, route, d], cr.at[section - 1, chain, route, d], device,
                )
            )

        @pl.when(has_next & (tile % 2 == 0))
        def _():
            for i, d in enumerate(FAR + (0,)):
                direct(i, d, SIDE)

        for plane in range(planes - 1):

            @pl.when(tile == 2 * plane + 1)
            def _():
                count = share(plane, section)
                for i, d in enumerate(FAR):
                    place = pl.ds(i * SIDE + count, SIDE - count)
                    act(
                        remote(
                            sent_next[chain][route].at[place],
                            passed[section - 1][chain][route].at[place],
                            ps.at[chain, route, d], pr.at[section - 1, chain, route, d],
                            {"tile": tile + 2},
                        )
                    )
                for i, d in enumerate(FAR + (0,)):
                    direct(i, d, count if d else SIDE)

    def pass_next(section, chain, start):
        for plane in range(planes - 1):

            @pl.when(tile == 2 * plane + 3)
            def _():
                count = share(plane, section)
                for i, d in enumerate(FAR):
                    for route in range(2):
                        src = passed[section - 1][chain][route].at[
                            pl.ds(i * SIDE + count, SIDE - count)
                        ]
                        if start:
                            arrived(src, pr.at[section - 1, chain, route, d])
                        copy = remote(
                            src,
                            cross[section - 1][chain][route].at[
                                pl.ds(d * SIDE + count, SIDE - count)
                            ],
                            qs.at[chain, route, d], qr.at[section - 1, chain, route, d],
                            {"tile": tile - 1, "lvl": across(route, d)},
                        )
                        if start:
                            copy.start()
                        else:
                            copy.wait_send()

    def hand_same(section, chain, route, start, readers=FAR):
        p = section % 2
        size = SIDE * CAP
        for d in readers:
            i = FAR.index(d)
            copy = remote(
                sent_same[chain][route].at[pl.ds(i * size, size)],
                got[p][chain][route].at[pl.ds(d * size, size)],
                hs.at[chain, route, d], hr.at[p, chain, route, d],
                {"lvl": across(route, d)},
            )
            if start:
                copy.start()
            else:
                copy.wait_send()

    def received(section, chain):
        p = section % 2
        size = SIDE * CAP
        for route in range(2):
            for d in FAR:
                arrived(
                    got[p][chain][route].at[pl.ds(d * size, size)], hr.at[p, chain, route, d]
                )

        def prior(d, begin, count, sems):
            for route in range(2):
                arrived(
                    cross[section - 1][chain][route].at[pl.ds(d * SIDE + begin, count)],
                    sems.at[section - 1, chain, route, d],
                )

        @pl.when(tile % 2 == 1)
        def _():
            for d in range(SIDE):
                prior(d, 0, SIDE, cr)

        for plane in range(planes - 1):

            @pl.when(tile == 2 * plane + 2)
            def _():
                count = share(plane, section)
                prior(0, 0, SIDE, cr)
                for d in FAR:
                    prior(d, 0, count, cr)
                    prior(d, count, SIDE - count, qr)

    def output(level):
        return [
            pltpu.make_async_copy(
                held[level][chain][route][0],
                out_ref.at[level, :, pl.ds(route * tall, tall), pl.ds(chain * wide, wide)],
                out_sem.at[level, chain, route],
            )
            for chain in range(2)
            for route in range(2)
        ]

    def write_last(chain, k):
        columns = pl.ds(chain * wide, wide)
        return pltpu.make_async_copy(
            last.at[part(k), :, columns], out_ref.at[depth - 1, part(k), :, columns],
            out_sem.at[depth - 1, chain, k],
        )

    def mix(section, chain):
        p = section % 2

        def one(k, carry):
            total = base[k, :, chain * wide : (chain + 1) * wide]
            for slot in range(NPAR):
                code = codes[section - 1, k * NPAR + slot]
                kind = lax.div(code, 65536)
                halves = []
                for route in range(2):
                    place = lax.rem(code if route == 0 else lax.div(code, 256), 256)
                    same = got[p][chain][route][lax.rem(place, CAP * peers)]
                    prior = cross[section - 1][chain][route][lax.rem(lax.div(place, CAP), peers)]
                    value = jnp.where(kind == 2, prior, same)
                    halves.append(jnp.where(kind == 0, jnp.zeros_like(value), value))
                parent = jnp.concatenate(halves, axis=0)
                total = total + jnp.dot(
                    fac[k, slot], parent, preferred_element_type=jnp.float32
                )
            value = total.astype(jnp.bfloat16)
            if section < depth - 1:
                keep(section, chain, k, value)
            else:
                last[k, :, chain * wide : (chain + 1) * wide] = value
            return carry

        return one

    for section in range(1, depth):
        level = section - 1
        for chain in range(2):
            forward(level, chain, True)
        if section == 1:
            lists[0] = asked[...]
            for route in range(2):
                for d in FAR:
                    arrived(asked, list_r.at[peer(route, d)])

            @pl.when(has_next)
            def _():
                for n in range(7):
                    arrived(asked, list_r.at[7 + n])

            @pl.when(jnp.logical_not(has_next))
            def _():
                for n in range(7):
                    lists[7 + n] = asked[...]

            copy = pltpu.make_async_copy(lists, table, table_sem)
            copy.start()
            copy.wait()
        for chain in range(2):
            if section > 1:
                for route in range(2):
                    hand_next(section - 1, chain, route, False)
                    hand_same(section - 1, chain, route, False)
                pass_next(section - 1, chain, False)
            gathered(level, chain)
            for route in range(2):
                build(section, chain, route)
            for route in range(2):
                hand_next(section, chain, route, True)
            if chain == 0:
                for route in range(2):
                    hand_same(section, 0, route, True, FAR[:1])
        pass_next(section, 0, True)
        for route in range(2):
            hand_same(section, 0, route, True, FAR[1:])
        pass_next(section, 1, True)
        for route in range(2):
            hand_same(section, 1, route, True)

        if section == 1:

            def encode(n, carry):
                for s in range(1, depth):
                    valid, prior, owner, local = entry(s, n)
                    dx = lax.rem(ix - lax.div(owner, SIDE) + SIDE, SIDE)
                    dy = lax.rem(iy - lax.rem(owner, SIDE) + SIDE, SIDE)
                    slot = jnp.where(table[0, 0, s - 1, owner] == local, 0, 1)
                    near = (dy * SIDE + dx) * CAP + slot
                    turned = (dx * SIDE + dy) * CAP + slot
                    kind = jnp.where(valid, jnp.where(prior, 2, 1), 0)
                    codes[s - 1, n] = near + 256 * turned + 65536 * kind
                return carry

            lax.fori_loop(0, blocks * NPAR, encode, 0)

        for copy in load_level(section):
            copy.wait()

        def own(k, carry):
            base[k] = product(section, k)
            return carry

        lax.fori_loop(0, blocks, own, 0, unroll=4)
        if section + 2 < depth:
            for copy in load_level(section + 2):
                copy.start()
        for copy in output(level):
            copy.start()
        for chain in range(2):
            sent_on(level, chain)
        load_factors(section).wait()
        for chain in range(2):
            received(section, chain)
            for k in range(PIECES):
                lax.fori_loop(k * piece, (k + 1) * piece, mix(section, chain), 0, unroll=4)
                if section < depth - 1:
                    spread(section, chain, k)
                else:
                    write_last(chain, k).start()
        if section < depth - 1:
            load_factors(section + 1).start()

    for chain in range(2):
        for route in range(2):
            hand_next(depth - 1, chain, route, False)
            hand_same(depth - 1, chain, route, False)
        pass_next(depth - 1, chain, False)
    for copy in list_copies(0):
        copy.wait_send()

    @pl.when(has_prior)
    def _():
        for copy in list_copies(1):
            copy.wait_send()

    for level in range(depth - 1):
        for copy in output(level):
            copy.wait()
    for chain in range(2):
        for k in range(PIECES):
            write_last(chain, k).wait()


def settle(src, dst, hold, in_sem, out_sem):
    depth, blocks = src.shape[:2]
    parts = [
        (level, k, pl.ds(k * (blocks // 4), blocks // 4))
        for level in range(depth)
        for k in range(4)
    ]
    for level, k, part in parts:
        pltpu.make_async_copy(
            src.at[level, part], hold.at[level, part], in_sem.at[level, k]
        ).start()
    for level, k, part in parts:
        pltpu.make_async_copy(
            src.at[level, part], hold.at[level, part], in_sem.at[level, k]
        ).wait()
        pltpu.make_async_copy(
            hold.at[level, part], dst.at[level, part], out_sem.at[level, k]
        ).start()
    for level, k, part in parts:
        pltpu.make_async_copy(
            hold.at[level, part], dst.at[level, part], out_sem.at[level, k]
        ).wait()


def shards(parents, factors, chol, noise):
    tiles = lax.axis_size("tile")
    depth, blocks, rows, _ = chol.shape
    real = noise.shape[3]
    peers = SIDE * SIDE

    def vmem(*shape, dtype=jnp.bfloat16):
        return pltpu.VMEM(shape, dtype)

    def half(count):
        return vmem(count, rows // 2, real // 2)

    def pairs(make):
        return [[make() for _ in range(2)] for _ in range(2)]

    dma = pltpu.SemaphoreType.DMA
    scratch = [
        [pairs(lambda: [half(blocks) for _ in range(SIDE)]) for _ in range(depth - 1)],
        [pairs(lambda: half(peers * CAP)) for _ in range(2)],
        [pairs(lambda: half(peers)) for _ in range(depth - 1)],
        [pairs(lambda: half(3 * SIDE)) for _ in range(depth - 1)],
        pairs(lambda: half(3 * SIDE * CAP)),
        pairs(lambda: half(4 * SIDE)),
        vmem(blocks, NPAR, rows, rows),
        vmem(2, blocks, rows, rows),
        vmem(2, blocks, rows, real),
        vmem(blocks, rows, real, dtype=jnp.float32),
        vmem(blocks, rows, real),
        vmem(3, 8, 128, dtype=jnp.int32),
        vmem(14, 3, 8, 128, dtype=jnp.int32),
        pltpu.SMEM((14, 3, 8, 128), jnp.int32),
        pltpu.SMEM((depth - 1, blocks * NPAR), jnp.int32),
        dma((2, 2, 2, 2, PIECES)), dma((2, 2, 2, 2, PIECES)),
        dma((2, 2, 2, 2)), dma((2, 2, 2, 2)),
        dma((2, 2, SIDE)), dma((2, 2, 2, SIDE)),
        dma((2, 2, SIDE)), dma((depth - 1, 2, 2, SIDE)),
        dma((2, 2, SIDE)), dma((depth - 1, 2, 2, SIDE)),
        dma((2, 2, SIDE)), dma((depth - 1, 2, 2, SIDE)),
        dma((14,)), dma((14,)),
        dma((5,)), dma((depth, 2, 2)), dma,
    ]
    flat, tree = jax.tree.flatten(scratch)

    def body(*refs):
        operands, rest = refs[:5], refs[5:]
        kernel(
            (depth, blocks, rows, real, tiles), *operands, *jax.tree.unflatten(tree, rest)
        )

    anywhere = pl.BlockSpec(memory_space=pl.ANY)
    field = pl.pallas_call(
        body,
        out_shape=jax.ShapeDtypeStruct((depth, blocks, rows, real), jnp.bfloat16),
        in_specs=[pl.BlockSpec(memory_space=pltpu.SMEM), anywhere, anywhere, anywhere],
        out_specs=anywhere,
        scratch_shapes=flat,
        compiler_params=pltpu.CompilerParams(
            collective_id=0, has_side_effects=True, vmem_limit_bytes=67043328
        ),
        name="field",
    )(parents.transpose(0, 2, 1), factors, chol, noise)
    return pl.pallas_call(
        settle,
        out_shape=jax.ShapeDtypeStruct(field.shape, field.dtype),
        in_specs=[anywhere],
        out_specs=anywhere,
        scratch_shapes=[
            vmem(*field.shape), dma((depth, 4)), dma((depth, 4)),
        ],
        name="settle",
    )(field)


def solution(mesh):
    placed = (
        P(None, ("tile", "lvl"), None),
        P(None, ("tile", "lvl"), None, None, None),
        P(None, ("tile", "lvl"), None, None),
        P(None, ("tile", "lvl"), None, None),
    )
    return jax.shard_map(
        shards,
        mesh=mesh,
        in_specs=placed,
        out_specs=P(None, ("tile", "lvl"), None, None),
        check_vma=False,
    )
```
